512 devices in a mesh: section: 2 (over core), sy: 8 (over y), sx: 8 (over z), mb: 4 (over x).
Axes of the slice: x: 4, y: 8, z: 8, core: 2. Of those that a mesh axis runs over, the one named last changes fastest.
Arguments:
- frames: bfloat16 [4, 512, 512, 128], P('mb', 'sy', 'sx'), may hold values from -6 to 6
- encode_weight: bfloat16 [512, 384], replicated, may hold values from -0.25 to 0.25
- conv_weight: bfloat16 [2, 1, 3456, 384], P('section', None, ('sy', 'sx')), may hold values from -0.109375 to 0.109375
- norm_gain: float32 [2, 1, 384], P('section'), may hold values from 0.1 to 1.9
- head_weight: bfloat16 [384, 256], replicated, may hold values from -0.3125 to 0.3125
- prior_logits: bfloat16 [4, 256, 256, 256], P('mb', 'sy', 'sx'), may hold values from -12 to 249
- target_bins: int32 [4, 256, 256], P('mb', 'sy', 'sx'), may hold values from 0 to 255
Outputs:
- section_features: bfloat16 [2, 4, 256, 256, 384], P('section', 'mb', 'sy', 'sx')
- head_step: float32 [384, 256], P('section')
- mean_loss: float32 [], replicated
The draws below stay inside these ranges and needn't reach their ends.
All inputs are finite; a program needn't handle non-finite values.
Results may differ from the reference program's by a relative error of at most 0.008.
Values may be sent and summed in bfloat16 or wider, within the bound.
No kernel may reach another device: no remote copies, remote signals or barrier semaphores. Data moves between devices by JAX's collectives and lax.ppermute only.
A program may use at most 64 MiB of HBM per device.

```python
import jax
import jax.numpy as jnp
from jax import lax

CH = 384
CIN = 128
BINS = 256
FIRST_DILATION = 1
LAYERS = 1
SAMPLES = 4
ENCODED_ROWS = 256
GRID_X = 256
N_SY = 8
N_SX = 8


def draw_prior_logits(key, part):
    full_shape = (SAMPLES, ENCODED_ROWS, GRID_X, BINS)
    key_base = jax.random.fold_in(key, 0)
    values = jnp.clip(3.0 * jax.random.normal(key_base, full_shape, jnp.float32), -12.0, 12.0)
    return values.astype(jnp.bfloat16)


def plant(result, stream_key, smallest, largest):
    shape = result.shape
    spot = [jax.random.randint(jax.random.fold_in(stream_key, axis), (), 0, shape[axis]) for axis in range(len(shape))]
    result = result.at[tuple(spot)].set(smallest)
    longest = shape.index(max(shape))
    spot[longest] = (spot[longest] + 1) % shape[longest]
    return result.at[tuple(spot)].set(largest)


def level_of(key, dims, pieces, low, high):
    level = 1.0
    for axis_at, parts in pieces:
        heights = jax.random.uniform(jax.random.fold_in(jax.random.fold_in(key, 6), axis_at), (parts,), jnp.float32, low / len(pieces), high / len(pieces))
        level = level * jnp.repeat(jnp.exp(heights), dims[axis_at] // parts).reshape((-1,) + (1,) * (len(dims) - 1 - axis_at))
    return level


def scatter_about(stream_key, shape, width, limit, cuts=(), dtype=jnp.bfloat16):
    factor_of = level_of(stream_key, shape, cuts, -0.22, 0.18) if cuts else 1.0
    drawn = jax.random.normal(stream_key, shape, jnp.float32) * width * factor_of
    return jnp.minimum(jnp.maximum(drawn, -limit), limit).astype(dtype)


def setup_inputs(seed: int = 0) -> dict:
    splits = jax.random.split(jax.random.key(seed), 8)
    return {
        "frames": scatter_about(splits[0], (SAMPLES, 2 * ENCODED_ROWS, 2 * GRID_X, CIN), 1.0, 6.0, ((0, 4), (1, 8), (2, 8))),
        "encode_weight": scatter_about(splits[1], (4 * CIN, CH), (4 * CIN) ** -0.5, 0.25),
        "conv_weight": scatter_about(splits[2], (2, LAYERS, 9 * CH, CH), (9 * CH) ** -0.5, 0.109375, ((0, 2), (2, 64))),
        "norm_gain": jnp.clip(1.0 + 0.18 * jax.random.normal(splits[3], (2, LAYERS, CH), jnp.float32), 0.1, 1.9),
        "head_weight": scatter_about(splits[4], (CH, BINS), CH ** -0.5, 0.3125),
        "prior_logits": draw_prior_logits(jax.random.fold_in(splits[7], 71), 0),
        "target_bins": plant(jax.random.randint(splits[6], (SAMPLES, ENCODED_ROWS, GRID_X), 0, BINS), jax.random.fold_in(splits[6], 1), 0, BINS - 1).astype(jnp.int32),
    }


def norm_gelu(activations, gain):
    values = activations.astype(jnp.float32)
    center = lax.optimization_barrier(jnp.mean(values, axis=-1, keepdims=True))
    offset = values - center
    spread = lax.optimization_barrier(jnp.mean(offset * offset, axis=-1, keepdims=True))
    normed = offset * lax.rsqrt(spread + 1e-05) * gain
    return jax.nn.gelu(normed, approximate=False).astype(jnp.bfloat16)

def dilated_filter(hidden, weight, step_y, step_x):
    height, across, channels = hidden.shape
    padded = jnp.pad(hidden, ((step_y, step_y), (step_x, step_x), (0, 0)))
    summed = jnp.zeros((height * across, weight.shape[1]), jnp.float32)
    for tap_row in range(3):
        for tap_column in range(3):
            window = padded[tap_row * step_y:tap_row * step_y + height, tap_column * step_x:tap_column * step_x + across]
            row_start = (tap_row * 3 + tap_column) * channels
            summed = summed + jnp.dot(window.reshape(height * across, channels), weight[row_start:row_start + channels], preferred_element_type=jnp.float32)
    return summed.reshape(height, across, weight.shape[1])

def reference(frames, encode_weight, conv_weight, norm_gain, head_weight, prior_logits, target_bins):

    def one_sample(inputs):
        frame, prior_rows, target = inputs
        blocks = frame.reshape(ENCODED_ROWS, 2, GRID_X, 2, CIN).astype(jnp.float32)
        kernel = encode_weight.reshape(2, 2, CIN, CH).astype(jnp.float32)
        activations = jnp.einsum('apbqc,pqco->abo', blocks, kernel).astype(jnp.bfloat16)
        outputs = []
        for section_index in range(2):
            for current_layer_index in range(LAYERS):
                starting_stride = FIRST_DILATION * 2 ** current_layer_index
                step_y = starting_stride * N_SY if section_index == 1 else starting_stride
                step_x = starting_stride * N_SX if section_index == 1 else starting_stride
                hidden = norm_gelu(activations, norm_gain[section_index, current_layer_index])
                branch = dilated_filter(hidden, conv_weight[section_index, current_layer_index], step_y, step_x)
                activations = (activations.astype(jnp.float32) + branch).astype(jnp.bfloat16)
            outputs.append(activations)
        flat_rows = activations.reshape(ENCODED_ROWS * GRID_X, CH)
        logits = jnp.dot(flat_rows, head_weight, preferred_element_type=jnp.float32)
        logits = logits + prior_rows.reshape(ENCODED_ROWS * GRID_X, BINS).astype(jnp.float32)
        row_top = lax.optimization_barrier(jnp.max(logits, axis=1, keepdims=True))
        shifted = logits - row_top
        exp_terms = jnp.exp(shifted)
        exp_total = lax.optimization_barrier(jnp.sum(exp_terms, axis=1, keepdims=True))
        softmax_rows = exp_terms / exp_total
        onehot = (target.reshape(ENCODED_ROWS * GRID_X, 1) == lax.broadcasted_iota(jnp.int32, (1, BINS), 1)).astype(jnp.float32)
        loss_sum = jnp.sum(jnp.log(exp_total[:, 0]) - lax.optimization_barrier(jnp.sum(shifted * onehot, axis=1)))
        delta_rows = (softmax_rows - onehot).astype(jnp.bfloat16)
        grad_part = jnp.dot(flat_rows.T, delta_rows, preferred_element_type=jnp.float32)
        return (outputs[0], outputs[1], grad_part, loss_sum)
    first_out, second_out, grads, losses = lax.map(one_sample, (frames, prior_logits, target_bins))
    gradient = lax.optimization_barrier(jnp.sum(grads, axis=0))
    head_step = gradient * lax.rsqrt(jnp.mean(gradient * gradient) + 1e-06)
    mean_loss = jnp.sum(losses) / (SAMPLES * ENCODED_ROWS * GRID_X)
    return (jnp.stack([first_out, second_out]), head_step, mean_loss)
```

```python
import jax
import jax.numpy as jnp
from jax import lax
from jax.sharding import PartitionSpec as P

FIRST_DILATION = 1
SECTION_FACTOR = 8


def norm_gelu(activations, gain):
    values = activations.astype(jnp.float32)
    center = jnp.mean(values, axis=-1, keepdims=True)
    offset = values - center
    spread = jnp.mean(offset * offset, axis=-1, keepdims=True)
    normed = offset * lax.rsqrt(spread + 1e-05) * gain
    return jax.nn.gelu(normed, approximate=False).astype(jnp.bfloat16)


def copies_to(block, axes, count):
    return lax.all_to_all(
        jnp.broadcast_to(block[None], (count,) + block.shape), axes, split_axis=0, concat_axis=0, tiled=True
    )


def swap(block):
    return lax.ppermute(block, "section", [(0, 1), (1, 0)])


def patches_of(padded, rows, columns, step):
    channels = padded.shape[-1]
    windows = [
        padded[i * step : i * step + rows, j * step : j * step + columns] for i in range(3) for j in range(3)
    ]
    return jnp.concatenate(windows, axis=2).reshape(rows * columns, 9 * channels)


def split_two(value):
    high = value.astype(jnp.bfloat16)
    low = (value - high.astype(jnp.float32)).astype(jnp.bfloat16)
    return high, low


def per_device(
    frames, encode_weight, conv_weight, norm_gain, head_weight, prior_logits, target_bins
):
    section = lax.axis_index("section")
    first = section == 0
    parts_y = lax.axis_size("sy")
    parts_x = lax.axis_size("sx")
    parts_b = lax.axis_size("mb")
    side = frames.shape[1] // 2
    half = side // 2
    channels = encode_weight.shape[1]
    bins = head_weight.shape[1]
    near = FIRST_DILATION
    far = FIRST_DILATION * SECTION_FACTOR
    reach = near + far

    shard = conv_weight[0, 0]
    strip = copies_to(shard, "sx", parts_x).reshape(parts_x * shard.shape[0], channels)
    weight_own = lax.all_gather(strip, "sy", axis=0, tiled=True)
    gain_own = norm_gain[0, 0]
    gain_other = swap(gain_own)
    gain_0 = jnp.where(first, gain_own, gain_other)
    gain_1 = jnp.where(first, gain_other, gain_own)

    blocks = frames[0].reshape(side, 2, side, 2, frames.shape[3])
    kernel = encode_weight.reshape(2, 2, frames.shape[3], channels)
    encoded = jnp.einsum(
        "apbqc,pqco->abo", blocks, kernel, preferred_element_type=jnp.float32
    ).astype(jnp.bfloat16)

    outgoing = jnp.where(first, encoded[side - reach :], encoded[:reach])
    route = [(y, y + 1) for y in range(parts_y - 1)] + [
        (parts_y + y + 1, parts_y + y) for y in range(parts_y - 1)
    ]
    arrived = lax.ppermute(outgoing, ("section", "sy"), route)
    rows = jnp.where(
        first,
        jnp.concatenate([arrived, encoded[: half + reach]], axis=0),
        jnp.concatenate([encoded[half - reach :], arrived], axis=0),
    )
    forward = [(x, x + 1) for x in range(parts_x - 1)]
    backward = [(x + 1, x) for x in range(parts_x - 1)]
    left = lax.ppermute(rows[:, side - reach :], "sx", forward)
    right = lax.ppermute(rows[:, :reach], "sx", backward)
    haloed = jnp.concatenate([left, rows, right], axis=1)

    tall, wide = half + 2 * far, side + 2 * far
    hidden = norm_gelu(haloed, gain_0)
    patches = patches_of(hidden, tall, wide, near)
    weight_own, patches = lax.optimization_barrier((weight_own, patches))
    weight_other = swap(weight_own)
    weight_0 = jnp.where(first, weight_own, weight_other)
    weight_1 = jnp.where(first, weight_other, weight_own)
    summed = jnp.dot(patches, weight_0, preferred_element_type=jnp.float32)
    features_0 = (
        haloed[near : near + tall, near : near + wide].astype(jnp.float32)
        + summed.reshape(tall, wide, channels)
    ).astype(jnp.bfloat16)

    row_at = lax.axis_index("sy") * side + section * half - far + lax.broadcasted_iota(jnp.int32, (tall, wide, 1), 0)
    column_at = lax.axis_index("sx") * side - far + lax.broadcasted_iota(jnp.int32, (tall, wide, 1), 1)
    inside = (row_at >= 0) & (row_at < side * parts_y) & (column_at >= 0) & (column_at < side * parts_x)
    hidden = jnp.where(inside, norm_gelu(features_0, gain_1), jnp.bfloat16(0))
    patches = patches_of(hidden, half, side, far)
    summed = jnp.dot(patches, weight_1, preferred_element_type=jnp.float32)
    own_0 = features_0[far : far + half, far : far + side]
    own_1 = (own_0.astype(jnp.float32) + summed.reshape(half, side, channels)).astype(jnp.bfloat16)

    cells = half * side
    flat = own_1.reshape(cells, channels)
    prior = lax.dynamic_slice_in_dim(prior_logits[0], section * half, half, axis=0)
    target = lax.dynamic_slice_in_dim(target_bins[0], section * half, half, axis=0)
    logits = jnp.dot(flat, head_weight, preferred_element_type=jnp.float32)
    logits = logits + prior.reshape(cells, bins).astype(jnp.float32)
    row_top = jnp.max(logits, axis=1, keepdims=True)
    shifted = logits - row_top
    exp_terms = jnp.exp(shifted)
    exp_total = jnp.sum(exp_terms, axis=1, keepdims=True)
    softmax_rows = exp_terms / exp_total
    onehot = (
        target.reshape(cells, 1) == lax.broadcasted_iota(jnp.int32, (1, bins), 1)
    ).astype(jnp.float32)
    loss_sum = jnp.sum(jnp.log(exp_total[:, 0]) - jnp.sum(shifted * onehot, axis=1))
    delta_rows = (softmax_rows - onehot).astype(jnp.bfloat16)
    gradient = lax.dot_general(
        flat, delta_rows, (((0,), (0,)), ((), ())), preferred_element_type=jnp.float32
    )

    slots = parts_x * parts_b
    slot_rows = channels // slots

    def with_loss(values, loss):
        high, low = split_two(loss)
        lane = lax.broadcasted_iota(jnp.int32, (1, bins), 1)
        row = jnp.where(lane == 0, high, jnp.where(lane == 1, low, jnp.bfloat16(0)))
        row = jnp.broadcast_to(row, values.shape[:-2] + (1, bins))
        return jnp.concatenate([values.astype(jnp.bfloat16), row], axis=-2)

    packed = with_loss(gradient.reshape(slots, slot_rows, bins), loss_sum)
    packed = lax.all_to_all(packed, ("sx", "mb"), split_axis=0, concat_axis=0, tiled=True)
    partial = jnp.sum(packed.astype(jnp.float32), axis=0)
    packed = with_loss(partial[:slot_rows], partial[slot_rows, 0] + partial[slot_rows, 1])
    packed = copies_to(packed, ("section", "sy"), 2 * parts_y)
    partial = jnp.sum(packed.astype(jnp.float32), axis=0)
    loss_all = partial[slot_rows, 0] + partial[slot_rows, 1]
    gathered = copies_to(partial[:slot_rows].astype(jnp.bfloat16), ("sx", "mb"), slots)
    gradient = gathered.reshape(channels, bins).astype(jnp.float32)
    scale = lax.rsqrt(jnp.mean(gradient * gradient) + 1e-06)
    own_rows = lax.dynamic_slice_in_dim(gradient, section * (channels // 2), channels // 2, axis=0)
    head_step = own_rows * scale
    mean_loss = loss_all / (parts_b * parts_y * parts_x * side * side)

    sent = swap(jnp.where(first, own_1, own_0))
    stacked = jnp.where(
        first, jnp.concatenate([own_0, sent], axis=0), jnp.concatenate([sent, own_1], axis=0)
    )[None, None]
    return (stacked, head_step, mean_loss)


def solution(mesh):
    placed = (
        P("mb", "sy", "sx", None),
        P(),
        P("section", None, ("sy", "sx"), None),
        P("section", None, None),
        P(),
        P("mb", "sy", "sx", None),
        P("mb", "sy", "sx"),
    )
    return jax.shard_map(
        per_device,
        mesh=mesh,
        in_specs=placed,
        out_specs=(P("section", "mb", "sy", "sx", None), P("section", None), P()),
        check_vma=False,
    )
```

```python
import functools

import jax
import jax.numpy as jnp
from jax import lax
from jax.experimental import pallas as pl
from jax.experimental.pallas import tpu as pltpu
from jax.sharding import PartitionSpec as P

FIRST_DILATION = 1
SECTION_FACTOR = 8


def norm_gelu(activations, gain):
    values = activations.astype(jnp.float32)
    center = jnp.mean(values, axis=-1, keepdims=True)
    offset = values - center
    spread = jnp.mean(offset * offset, axis=-1, keepdims=True)
    normed = offset * lax.rsqrt(spread + 1e-05) * gain
    return jax.nn.gelu(normed, approximate=False).astype(jnp.bfloat16)


def copies_to(block, axes, count):
    return lax.all_to_all(
        jnp.broadcast_to(block[None], (count,) + block.shape), axes, split_axis=0, concat_axis=0, tiled=True
    )


def swap(block):
    return lax.ppermute(block, "section", [(0, 1), (1, 0)])


def columns_of(padded, wide, step):
    return jnp.concatenate([padded[:, j * step : j * step + wide] for j in range(3)], axis=2)


def erf(value):
    top = 3.832506856900711
    value = jnp.clip(value, -top, top)
    square = value * value
    over = jnp.float32(0.00022905065861350646)
    for term in (0.0034082910107109506, 0.050955695062380861, 0.18520832239976145, 1.128379143519084):
        over = over * square + term
    under = jnp.float32(-1.1791602954361697e-7)
    for term in (
        0.000023547966471313185,
        0.0010179625278914885,
        0.014070470171167667,
        0.11098505178285362,
        0.49746925110067538,
        1.0,
    ):
        under = under * square + term
    return value * over / under


def layers_kernel(
    sizes,
    stacked_hbm,
    center_ref,
    own_ref,
    other_ref,
    gain_ref,
    head_ref,
    prior_ref,
    target_ref,
    out_0_ref,
    out_1_ref,
    packed_ref,
    stacked_ref,
    weight_0,
    weight_1,
    hidden_ref,
    sem_s,
    sem_0,
    sem_1,
):
    far, half, side, band, slots, parts_y, parts_x = sizes
    tall, wide, taps = stacked_ref.shape[0] - 2, stacked_ref.shape[1], stacked_ref.shape[2]
    channels = taps // 3
    bins = head_ref.shape[1]
    section = lax.axis_index("section")

    def strip(t):
        low = 0 if t == 0 else t * band + 2
        at = pl.ds(low, t * band + band + 2 - low)
        return pltpu.make_async_copy(stacked_hbm.at[at], stacked_ref.at[at], sem_s.at[t])

    strip(0).start()

    def fetch(source, target, sems):
        for i in range(3):
            at = pl.ds(i * taps, taps)
            pltpu.make_async_copy(source.at[at], target.at[at], sems.at[i]).start()

    @pl.when(section == 0)
    def _():
        fetch(own_ref, weight_0, sem_0)

    @pl.when(section != 0)
    def _():
        fetch(other_ref, weight_0, sem_0)

    for t in range(1, tall // band):
        strip(t).start()

    @pl.when(section == 0)
    def _():
        fetch(other_ref, weight_1, sem_1)

    @pl.when(section != 0)
    def _():
        fetch(own_ref, weight_1, sem_1)

    def arrive(target, sems, i):
        at = pl.ds(i * taps, taps)
        pltpu.make_async_copy(own_ref.at[at], target.at[at], sems.at[i]).wait()

    row_start = lax.axis_index("sy") * side + section * half - far
    column_at = lax.axis_index("sx") * side - far + lax.broadcasted_iota(jnp.int32, (band, wide, 1), 1)
    column_in = (column_at >= 0) & (column_at < side * parts_x)
    gain = gain_ref[...].reshape(1, 1, channels)
    for t in range(tall // band):
        strip(t).wait()
        total = jnp.zeros((band * wide, channels), jnp.float32)
        for i in range(3):
            if t == 0:
                arrive(weight_0, sem_0, i)
            total += jnp.dot(
                stacked_ref[t * band + i : t * band + i + band].reshape(band * wide, taps),
                weight_0[i * taps : (i + 1) * taps],
                preferred_element_type=jnp.float32,
            )
        total = total.reshape(band, wide, channels) + center_ref[t * band : (t + 1) * band].astype(jnp.float32)
        values = total.astype(jnp.bfloat16).astype(jnp.float32)
        if far <= t * band < far + half:
            out_0_ref[t * band - far : (t + 1) * band - far] = values[:, far : far + side].astype(jnp.bfloat16)
        mean = jnp.mean(values, axis=-1, keepdims=True)
        offset = values - mean
        spread = jnp.mean(offset * offset, axis=-1, keepdims=True)
        row_at = row_start + t * band + lax.broadcasted_iota(jnp.int32, (band, wide, 1), 0)
        inside = column_in & (row_at >= 0) & (row_at < side * parts_y)
        normed = offset * jnp.where(inside, lax.rsqrt(spread + 1e-05), 0.0) * gain
        active = 0.5 * normed * (1.0 + erf(normed * 0.7071067811865476))
        for j in range(3):
            hidden_ref[t * band : (t + 1) * band, :, j * channels : (j + 1) * channels] = active[
                :, j * far : j * far + side
            ].astype(jnp.bfloat16)

    cells = half * side
    total = jnp.zeros((cells, channels), jnp.float32)
    for i in range(3):
        arrive(weight_1, sem_1, i)
        total += jnp.dot(
            hidden_ref[i * far : i * far + half].reshape(cells, taps),
            weight_1[i * taps : (i + 1) * taps],
            preferred_element_type=jnp.float32,
        )
    flat = (total + out_0_ref[...].reshape(cells, channels).astype(jnp.float32)).astype(jnp.bfloat16)
    out_1_ref[...] = flat.reshape(half, side, channels)
    logits = jnp.dot(flat, head_ref[...], preferred_element_type=jnp.float32)
    logits = logits + prior_ref[...].astype(jnp.float32)
    shifted = logits - jnp.max(logits, axis=1, keepdims=True)
    exp_terms = jnp.exp(shifted)
    exp_total = jnp.sum(exp_terms, axis=1, keepdims=True)
    hit = target_ref[...] == lax.broadcasted_iota(jnp.int32, (cells, bins), 1)
    picked = jnp.sum(jnp.where(hit, shifted, 0.0), axis=1, keepdims=True)
    loss = jnp.sum(jnp.log(exp_total) - picked, axis=0, keepdims=True)
    delta = (exp_terms / exp_total - hit.astype(jnp.float32)).astype(jnp.bfloat16)
    gradient = lax.dot_general(
        flat, delta, (((0,), (0,)), ((), ())), preferred_element_type=jnp.float32
    )
    loss = jnp.broadcast_to(loss, (8, 128))
    deep = channels * bins // (128 * slots)
    across = channels // deep
    for s in range(slots):
        row, lane = (s % across) * deep, (s // across) * 128
        chunk = jnp.concatenate([gradient[row : row + deep, lane : lane + 128], loss], axis=0)
        packed_ref[s] = chunk.astype(jnp.bfloat16)


def per_device(
    frames, encode_weight, conv_weight, norm_gain, head_weight, prior_logits, target_bins
):
    section = lax.axis_index("section")
    first = section == 0
    parts_y = lax.axis_size("sy")
    parts_x = lax.axis_size("sx")
    parts_b = lax.axis_size("mb")
    side = frames.shape[1] // 2
    half = side // 2
    channels = encode_weight.shape[1]
    bins = head_weight.shape[1]
    near = FIRST_DILATION
    far = FIRST_DILATION * SECTION_FACTOR
    reach = near + far

    shard = conv_weight[0, 0]
    strip = copies_to(shard, "sx", parts_x)
    gain_own = norm_gain[0, 0]
    gain_other = swap(gain_own)
    gain_0 = jnp.where(first, gain_own, gain_other)
    gain_1 = jnp.where(first, gain_other, gain_own)

    blocks = frames[0].reshape(side, 2, side, 2, frames.shape[3])
    kernel = encode_weight.reshape(2, 2, frames.shape[3], channels)
    encoded = jnp.einsum(
        "apbqc,pqco->abo", blocks, kernel, preferred_element_type=jnp.float32
    ).astype(jnp.bfloat16)

    strip, encoded = lax.optimization_barrier((strip, encoded))
    weight_own = lax.all_gather(
        strip.reshape(parts_x * shard.shape[0], channels), "sy", axis=0, tiled=True
    )

    outgoing = jnp.where(first, encoded[side - reach :], encoded[:reach])
    route = [(y, y + 1) for y in range(parts_y - 1)] + [
        (parts_y + y + 1, parts_y + y) for y in range(parts_y - 1)
    ]
    arrived = lax.ppermute(outgoing, ("section", "sy"), route)
    rows = jnp.where(
        first,
        jnp.concatenate([arrived, encoded[: half + reach]], axis=0),
        jnp.concatenate([encoded[half - reach :], arrived], axis=0),
    )
    forward = [(x, x + 1) for x in range(parts_x - 1)]
    backward = [(x + 1, x) for x in range(parts_x - 1)]
    left = lax.ppermute(rows[:, side - reach :], "sx", forward)
    right = lax.ppermute(rows[:, :reach], "sx", backward)
    haloed = jnp.concatenate([left, rows, right], axis=1)

    tall, wide = half + 2 * far, side + 2 * far
    cells = half * side
    stacked = columns_of(norm_gelu(haloed, gain_0), wide, near)
    center = haloed[near : near + tall, near : near + wide]
    prior = lax.dynamic_slice_in_dim(prior_logits[0], section * half, half, axis=0).reshape(cells, bins)
    target = lax.dynamic_slice_in_dim(target_bins[0], section * half, half, axis=0).reshape(cells, 1)
    weight_own, stacked, center, prior, target = lax.optimization_barrier(
        (weight_own, stacked, center, prior, target)
    )
    weight_other = swap(weight_own)
    slots = parts_x * parts_b
    deep = channels * bins // (128 * slots)
    vmem = pl.BlockSpec(memory_space=pltpu.VMEM)
    anywhere = pl.BlockSpec(memory_space=pl.ANY)
    taps = 3 * channels
    own_0, own_1, packed = pl.pallas_call(
        functools.partial(layers_kernel, (far, half, side, 8, slots, parts_y, parts_x)),
        out_shape=(
            jax.ShapeDtypeStruct((half, side, channels), jnp.bfloat16),
            jax.ShapeDtypeStruct((half, side, channels), jnp.bfloat16),
            jax.ShapeDtypeStruct((slots, deep + 8, 128), jnp.bfloat16),
        ),
        in_specs=[anywhere, vmem, anywhere, anywhere, vmem, vmem, vmem, vmem],
        out_specs=(vmem, vmem, vmem),
        scratch_shapes=[
            pltpu.VMEM((tall + 2 * near, wide, taps), jnp.bfloat16),
            pltpu.VMEM((3 * taps, channels), jnp.bfloat16),
            pltpu.VMEM((3 * taps, channels), jnp.bfloat16),
            pltpu.VMEM((tall, side, taps), jnp.bfloat16),
            pltpu.SemaphoreType.DMA((tall // 8,)),
            pltpu.SemaphoreType.DMA((3,)),
            pltpu.SemaphoreType.DMA((3,)),
        ],
        compiler_params=pltpu.CompilerParams(vmem_limit_bytes=52 * 2**20),
        cost_estimate=pl.CostEstimate(
            flops=2 * (tall * wide + cells) * 3 * taps * channels,
            bytes_accessed=6 * taps * channels * 2,
            transcendentals=0,
        ),
    )(stacked, center, weight_own, weight_other, gain_1.reshape(1, channels), head_weight, prior, target)

    packed = lax.all_to_all(packed, ("sx", "mb"), split_axis=0, concat_axis=0, tiled=True)
    partial = jnp.sum(packed.astype(jnp.float32), axis=0).astype(jnp.bfloat16)
    packed = copies_to(partial, ("section", "sy"), 2 * parts_y)
    partial = jnp.sum(packed.astype(jnp.float32), axis=0)
    loss_all = partial[deep, 0]
    gathered = copies_to(partial[:deep].astype(jnp.bfloat16), ("sx", "mb"), slots)
    scale = lax.rsqrt(jnp.mean(jnp.square(gathered.astype(jnp.float32))) + 1e-06)
    halves = bins // 128
    by_half = gathered.reshape(halves, channels, 128)
    own_rows = lax.dynamic_slice_in_dim(by_half, section * (channels // 2), channels // 2, axis=1)
    head_step = jnp.concatenate(
        [own_rows[h].astype(jnp.float32) * scale for h in range(halves)], axis=1
    )
    mean_loss = loss_all / (parts_b * parts_y * parts_x * side * side)

    sent = swap(jnp.where(first, own_1, own_0))
    grids = jnp.where(
        first, jnp.concatenate([own_0, sent], axis=0), jnp.concatenate([sent, own_1], axis=0)
    )[None, None]
    return (grids, head_step, mean_loss)


def solution(mesh):
    placed = (
        P("mb", "sy", "sx", None),
        P(),
        P("section", None, ("sy", "sx"), None),
        P("section", None, None),
        P(),
        P("mb", "sy", "sx", None),
        P("mb", "sy", "sx"),
    )
    return jax.shard_map(
        per_device,
        mesh=mesh,
        in_specs=placed,
        out_specs=(P("section", "mb", "sy", "sx", None), P("section", None), P()),
        check_vma=False,
    )
```

```python
import functools

import jax
import jax.numpy as jnp
from jax import lax
from jax.experimental import pallas as pl
from jax.experimental.pallas import tpu as pltpu
from jax.sharding import PartitionSpec as P

FIRST_DILATION = 1
SECTION_FACTOR = 8


def norm_gelu(activations, gain):
    values = activations.astype(jnp.float32)
    center = jnp.mean(values, axis=-1, keepdims=True)
    offset = values - center
    spread = jnp.mean(offset * offset, axis=-1, keepdims=True)
    normed = offset * lax.rsqrt(spread + 1e-05) * gain
    return jax.nn.gelu(normed, approximate=False).astype(jnp.bfloat16)


def copies_to(block, axes, count):
    return lax.all_to_all(
        jnp.broadcast_to(block[None], (count,) + block.shape), axes, split_axis=0, concat_axis=0, tiled=True
    )


def swap(block):
    return lax.ppermute(block, "section", [(0, 1), (1, 0)])


def columns_of(padded, wide, step):
    return jnp.concatenate([padded[:, j * step : j * step + wide] for j in range(3)], axis=2)


def erf(value):
    top = 3.832506856900711
    value = jnp.clip(value, -top, top)
    square = value * value
    over = jnp.float32(0.00022905065861350646)
    for term in (0.0034082910107109506, 0.050955695062380861, 0.18520832239976145, 1.128379143519084):
        over = over * square + term
    under = jnp.float32(-1.1791602954361697e-7)
    for term in (
        0.000023547966471313185,
        0.0010179625278914885,
        0.014070470171167667,
        0.11098505178285362,
        0.49746925110067538,
        1.0,
    ):
        under = under * square + term
    return value * over / under


def layers_kernel(
    sizes,
    stacked_hbm,
    center_ref,
    weights_ref,
    gain_ref,
    head_ref,
    prior_ref,
    target_ref,
    out_0_ref,
    out_1_ref,
    packed_ref,
    stacked_ref,
    weight_0,
    weight_1,
    hidden_ref,
    sem_s,
    sem_w,
):
    far, half, side, band, slots, parts_y, parts_x = sizes
    tall, wide, taps = stacked_ref.shape[0] - 2, stacked_ref.shape[1], stacked_ref.shape[2]
    channels = taps // 3
    bins = head_ref.shape[1]
    section = lax.axis_index("section")

    def strip(t):
        low = 0 if t == 0 else t * band + 2
        at = pl.ds(low, t * band + band + 2 - low)
        return pltpu.make_async_copy(stacked_hbm.at[at], stacked_ref.at[at], sem_s.at[t])

    strip(0).start()

    def weights(layer, target, sem):
        return pltpu.make_async_copy(weights_ref.at[pl.ds(layer * 3 * taps, 3 * taps)], target, sem)

    fetch_0, fetch_1 = weights(0, weight_0, sem_w.at[0]), weights(1, weight_1, sem_w.at[1])
    fetch_0.start()
    for t in range(1, tall // band):
        strip(t).start()
    fetch_1.start()

    row_start = lax.axis_index("sy") * side + section * half - far
    column_at = lax.axis_index("sx") * side - far + lax.broadcasted_iota(jnp.int32, (band, wide, 1), 1)
    column_in = (column_at >= 0) & (column_at < side * parts_x)
    gain = gain_ref[...].reshape(1, 1, channels)
    for t in range(tall // band):
        strip(t).wait()
        if t == 0:
            fetch_0.wait()
        total = jnp.dot(
            jnp.concatenate(
                [stacked_ref[t * band + i : t * band + i + band] for i in range(3)], axis=2
            ).reshape(band * wide, 3 * taps),
            weight_0[...],
            preferred_element_type=jnp.float32,
        )
        total = total.reshape(band, wide, channels) + center_ref[t * band : (t + 1) * band].astype(jnp.float32)
        values = total.astype(jnp.bfloat16).astype(jnp.float32)
        if far <= t * band < far + half:
            out_0_ref[t * band - far : (t + 1) * band - far] = values[:, far : far + side].astype(jnp.bfloat16)
        mean = jnp.mean(values, axis=-1, keepdims=True)
        offset = values - mean
        spread = jnp.mean(offset * offset, axis=-1, keepdims=True)
        row_at = row_start + t * band + lax.broadcasted_iota(jnp.int32, (band, wide, 1), 0)
        inside = column_in & (row_at >= 0) & (row_at < side * parts_y)
        normed = offset * jnp.where(inside, lax.rsqrt(spread + 1e-05), 0.0) * gain
        active = 0.5 * normed * (1.0 + erf(normed * 0.7071067811865476))
        for j in range(3):
            hidden_ref[t * band : (t + 1) * band, :, j * channels : (j + 1) * channels] = active[
                :, j * far : j * far + side
            ].astype(jnp.bfloat16)

    cells = half * side
    fetch_1.wait()
    total = jnp.dot(
        jnp.concatenate([hidden_ref[i * far : i * far + half] for i in range(3)], axis=2).reshape(cells, 3 * taps),
        weight_1[...],
        preferred_element_type=jnp.float32,
    )
    flat = (total + out_0_ref[...].reshape(cells, channels).astype(jnp.float32)).astype(jnp.bfloat16)
    out_1_ref[...] = flat.reshape(half, side, channels)
    logits = jnp.dot(flat, head_ref[...], preferred_element_type=jnp.float32)
    logits = logits + prior_ref[...].astype(jnp.float32)
    shifted = logits - jnp.max(logits, axis=1, keepdims=True)
    exp_terms = jnp.exp(shifted)
    exp_total = jnp.sum(exp_terms, axis=1, keepdims=True)
    hit = target_ref[...] == lax.broadcasted_iota(jnp.int32, (cells, bins), 1)
    picked = jnp.sum(jnp.where(hit, shifted, 0.0), axis=1, keepdims=True)
    loss = jnp.sum(jnp.log(exp_total) - picked, axis=0, keepdims=True)
    delta = (exp_terms / exp_total - hit.astype(jnp.float32)).astype(jnp.bfloat16)
    gradient = lax.dot_general(
        flat, delta, (((0,), (0,)), ((), ())), preferred_element_type=jnp.float32
    )
    loss = jnp.broadcast_to(loss, (8, 128))
    deep = channels * bins // (128 * slots)
    across = channels // deep
    for s in range(slots):
        row, lane = (s % across) * deep, (s // across) * 128
        chunk = jnp.concatenate([gradient[row : row + deep, lane : lane + 128], loss], axis=0)
        packed_ref[s] = chunk.astype(jnp.bfloat16)


def per_device(
    frames, encode_weight, conv_weight, norm_gain, head_weight, prior_logits, target_bins
):
    section = lax.axis_index("section")
    first = section == 0
    parts_y = lax.axis_size("sy")
    parts_x = lax.axis_size("sx")
    parts_b = lax.axis_size("mb")
    side = frames.shape[1] // 2
    half = side // 2
    channels = encode_weight.shape[1]
    bins = head_weight.shape[1]
    near = FIRST_DILATION
    far = FIRST_DILATION * SECTION_FACTOR
    reach = near + far

    shard = conv_weight[0, 0]
    strip = copies_to(shard, "sx", parts_x)
    strip, encode_weight, gain_own = lax.optimization_barrier((strip, encode_weight, norm_gain[0, 0]))
    weights = lax.all_gather(
        strip.reshape(parts_x * shard.shape[0], channels), ("section", "sy"), axis=0, tiled=True
    )
    gain_other = swap(gain_own)
    gain_0 = jnp.where(first, gain_own, gain_other)
    gain_1 = jnp.where(first, gain_other, gain_own)

    blocks = frames[0].reshape(side, 2, side, 2, frames.shape[3])
    kernel = encode_weight.reshape(2, 2, frames.shape[3], channels)
    encoded = jnp.einsum(
        "apbqc,pqco->abo", blocks, kernel, preferred_element_type=jnp.float32
    ).astype(jnp.bfloat16)

    outgoing = jnp.where(first, encoded[side - reach :], encoded[:reach])
    route = [(y, y + 1) for y in range(parts_y - 1)] + [
        (parts_y + y + 1, parts_y + y) for y in range(parts_y - 1)
    ]
    arrived = lax.ppermute(outgoing, ("section", "sy"), route)
    rows = jnp.where(
        first,
        jnp.concatenate([arrived, encoded[: half + reach]], axis=0),
        jnp.concatenate([encoded[half - reach :], arrived], axis=0),
    )
    forward = [(x, x + 1) for x in range(parts_x - 1)]
    backward = [(x + 1, x) for x in range(parts_x - 1)]
    left = lax.ppermute(rows[:, side - reach :], "sx", forward)
    right = lax.ppermute(rows[:, :reach], "sx", backward)
    haloed = jnp.concatenate([left, rows, right], axis=1)

    tall, wide = half + 2 * far, side + 2 * far
    cells = half * side
    stacked = columns_of(norm_gelu(haloed, gain_0), wide, near)
    center = haloed[near : near + tall, near : near + wide]
    prior = lax.dynamic_slice_in_dim(prior_logits[0], section * half, half, axis=0).reshape(cells, bins)
    target = lax.dynamic_slice_in_dim(target_bins[0], section * half, half, axis=0).reshape(cells, 1)
    slots = parts_x * parts_b
    deep = channels * bins // (128 * slots)
    vmem = pl.BlockSpec(memory_space=pltpu.VMEM)
    anywhere = pl.BlockSpec(memory_space=pl.ANY)
    taps = 3 * channels
    own_0, own_1, packed = pl.pallas_call(
        functools.partial(layers_kernel, (far, half, side, 8, slots, parts_y, parts_x)),
        out_shape=(
            jax.ShapeDtypeStruct((half, side, channels), jnp.bfloat16),
            jax.ShapeDtypeStruct((half, side, channels), jnp.bfloat16),
            jax.ShapeDtypeStruct((slots, deep + 8, 128), jnp.bfloat16),
        ),
        in_specs=[anywhere, vmem, anywhere, vmem, vmem, vmem, vmem],
        out_specs=(vmem, vmem, vmem),
        scratch_shapes=[
            pltpu.VMEM((tall + 2 * near, wide, taps), jnp.bfloat16),
            pltpu.VMEM((3 * taps, channels), jnp.bfloat16),
            pltpu.VMEM((3 * taps, channels), jnp.bfloat16),
            pltpu.VMEM((tall, side, taps), jnp.bfloat16),
            pltpu.SemaphoreType.DMA((tall // 8,)),
            pltpu.SemaphoreType.DMA((2,)),
        ],
        compiler_params=pltpu.CompilerParams(vmem_limit_bytes=52 * 2**20),
        cost_estimate=pl.CostEstimate(
            flops=2 * (tall * wide + cells) * 3 * taps * channels,
            bytes_accessed=6 * taps * channels * 2,
            transcendentals=0,
        ),
    )(stacked, center, weights, gain_1.reshape(1, channels), head_weight, prior, target)

    packed = lax.all_to_all(packed, ("sx", "mb"), split_axis=0, concat_axis=0, tiled=True)
    partial = jnp.sum(packed.astype(jnp.float32), axis=0).astype(jnp.bfloat16)
    packed = copies_to(partial, ("section", "sy"), 2 * parts_y)
    partial = jnp.sum(packed.astype(jnp.float32), axis=0)
    loss_all = partial[deep, 0]
    gathered = copies_to(partial[:deep].astype(jnp.bfloat16), ("sx", "mb"), slots)
    scale = lax.rsqrt(jnp.mean(jnp.square(gathered.astype(jnp.float32))) + 1e-06)
    halves = bins // 128
    by_half = gathered.reshape(halves, channels, 128)
    own_rows = lax.dynamic_slice_in_dim(by_half, section * (channels // 2), channels // 2, axis=1)
    head_step = jnp.concatenate(
        [own_rows[h].astype(jnp.float32) * scale for h in range(halves)], axis=1
    )
    mean_loss = loss_all / (parts_b * parts_y * parts_x * side * side)

    sent = swap(jnp.where(first, own_1, own_0))
    grids = jnp.where(
        first, jnp.concatenate([own_0, sent], axis=0), jnp.concatenate([sent, own_1], axis=0)
    )[None, None]
    return (grids, head_step, mean_loss)


def solution(mesh):
    placed = (
        P("mb", "sy", "sx", None),
        P(),
        P("section", None, ("sy", "sx"), None),
        P("section", None, None),
        P(),
        P("mb", "sy", "sx", None),
        P("mb", "sy", "sx"),
    )
    return jax.shard_map(
        per_device,
        mesh=mesh,
        in_specs=placed,
        out_specs=(P("section", "mb", "sy", "sx", None), P("section", None), P()),
        check_vma=False,
    )
```

```python
import functools

import jax
import jax.numpy as jnp
from jax import lax
from jax.experimental import pallas as pl
from jax.experimental.pallas import tpu as pltpu
from jax.sharding import PartitionSpec as P

FIRST_DILATION = 1
SECTION_FACTOR = 8


def norm_gelu(activations, gain):
    values = activations.astype(jnp.float32)
    center = jnp.mean(values, axis=-1, keepdims=True)
    offset = values - center
    spread = jnp.mean(offset * offset, axis=-1, keepdims=True)
    normed = offset * lax.rsqrt(spread + 1e-05) * gain
    return jax.nn.gelu(normed, approximate=False).astype(jnp.bfloat16)


def copies_to(block, axes, count):
    return lax.all_to_all(
        jnp.broadcast_to(block[None], (count,) + block.shape), axes, split_axis=0, concat_axis=0, tiled=True
    )


def swap(block):
    return lax.ppermute(block, "section", [(0, 1), (1, 0)])


def columns_of(padded, wide, step):
    return jnp.concatenate([padded[:, j * step : j * step + wide] for j in range(3)], axis=2)


def erf(value):
    top = 3.832506856900711
    value = jnp.clip(value, -top, top)
    square = value * value
    over = jnp.float32(0.00022905065861350646)
    for term in (0.0034082910107109506, 0.050955695062380861, 0.18520832239976145, 1.128379143519084):
        over = over * square + term
    under = jnp.float32(-1.1791602954361697e-7)
    for term in (
        0.000023547966471313185,
        0.0010179625278914885,
        0.014070470171167667,
        0.11098505178285362,
        0.49746925110067538,
        1.0,
    ):
        under = under * square + term
    return value * over / under


def layers_kernel(
    sizes,
    stacked_hbm,
    center_ref,
    weights_ref,
    gain_ref,
    head_ref,
    prior_ref,
    target_ref,
    out_0_ref,
    out_1_ref,
    packed_ref,
    stacked_ref,
    weight_0,
    weight_1,
    hidden_ref,
    sem_s,
    sem_w,
):
    far, half, side, band, slots, parts_y, parts_x = sizes
    tall, wide, taps = stacked_ref.shape[0] - 2, stacked_ref.shape[1], stacked_ref.shape[2]
    channels = taps // 3
    bins = head_ref.shape[1]
    section = lax.axis_index("section")

    def strip(t):
        low = 0 if t == 0 else t * band + 2
        at = pl.ds(low, t * band + band + 2 - low)
        return pltpu.make_async_copy(stacked_hbm.at[at], stacked_ref.at[at], sem_s.at[t])

    strip(0).start()

    def weights(layer, target, sem):
        return pltpu.make_async_copy(weights_ref.at[pl.ds(layer * 3 * taps, 3 * taps)], target, sem)

    fetch_0, fetch_1 = weights(0, weight_0, sem_w.at[0]), weights(1, weight_1, sem_w.at[1])
    fetch_0.start()
    for t in range(1, tall // band):
        strip(t).start()
    fetch_1.start()

    row_start = lax.axis_index("sy") * side + section * half - far
    column_at = lax.axis_index("sx") * side - far + lax.broadcasted_iota(jnp.int32, (band, wide, 1), 1)
    column_in = (column_at >= 0) & (column_at < side * parts_x)
    gain = gain_ref[...].reshape(1, 1, channels)
    fetch_0.wait()
    for t in range(tall // band):
        strip(t).wait()
    for t in range(tall // band):
        total = jnp.dot(
            jnp.concatenate(
                [stacked_ref[t * band + i : t * band + i + band] for i in range(3)], axis=2
            ).reshape(band * wide, 3 * taps),
            weight_0[...],
            preferred_element_type=jnp.float32,
        )
        total = total.reshape(band, wide, channels) + center_ref[t * band : (t + 1) * band].astype(jnp.float32)
        values = total.astype(jnp.bfloat16).astype(jnp.float32)
        if far <= t * band < far + half:
            out_0_ref[t * band - far : (t + 1) * band - far] = values[:, far : far + side].astype(jnp.bfloat16)
        mean = jnp.mean(values, axis=-1, keepdims=True)
        offset = values - mean
        spread = jnp.mean(offset * offset, axis=-1, keepdims=True)
        row_at = row_start + t * band + lax.broadcasted_iota(jnp.int32, (band, wide, 1), 0)
        inside = column_in & (row_at >= 0) & (row_at < side * parts_y)
        normed = offset * jnp.where(inside, lax.rsqrt(spread + 1e-05), 0.0) * gain
        active = 0.5 * normed * (1.0 + erf(normed * 0.7071067811865476))
        for j in range(3):
            hidden_ref[t * band : (t + 1) * band, :, j * channels : (j + 1) * channels] = active[
                :, j * far : j * far + side
            ].astype(jnp.bfloat16)

    cells = half * side
    fetch_1.wait()
    total = jnp.dot(
        jnp.concatenate([hidden_ref[i * far : i * far + half] for i in range(3)], axis=2).reshape(cells, 3 * taps),
        weight_1[...],
        preferred_element_type=jnp.float32,
    )
    flat = (total + out_0_ref[...].reshape(cells, channels).astype(jnp.float32)).astype(jnp.bfloat16)
    out_1_ref[...] = flat.reshape(half, side, channels)
    logits = jnp.dot(flat, head_ref[...], preferred_element_type=jnp.float32)
    logits = logits + prior_ref[...].astype(jnp.float32)
    shifted = logits - jnp.max(logits, axis=1, keepdims=True)
    exp_terms = jnp.exp(shifted)
    exp_total = jnp.sum(exp_terms, axis=1, keepdims=True)
    hit = target_ref[...] == lax.broadcasted_iota(jnp.int32, (cells, bins), 1)
    picked = jnp.sum(jnp.where(hit, shifted, 0.0), axis=1, keepdims=True)
    loss = jnp.sum(jnp.log(exp_total) - picked, axis=0, keepdims=True)
    delta = (exp_terms / exp_total - hit.astype(jnp.float32)).astype(jnp.bfloat16)
    gradient = lax.dot_general(
        flat, delta, (((0,), (0,)), ((), ())), preferred_element_type=jnp.float32
    )
    loss = jnp.broadcast_to(loss, (8, 128))
    deep = channels * bins // (128 * slots)
    across = channels // deep
    for s in range(slots):
        row, lane = (s % across) * deep, (s // across) * 128
        chunk = jnp.concatenate([gradient[row : row + deep, lane : lane + 128], loss], axis=0)
        packed_ref[s] = chunk.astype(jnp.bfloat16)


def per_device(
    frames, encode_weight, conv_weight, norm_gain, head_weight, prior_logits, target_bins
):
    section = lax.axis_index("section")
    first = section == 0
    parts_y = lax.axis_size("sy")
    parts_x = lax.axis_size("sx")
    parts_b = lax.axis_size("mb")
    side = frames.shape[1] // 2
    half = side // 2
    channels = encode_weight.shape[1]
    bins = head_weight.shape[1]
    near = FIRST_DILATION
    far = FIRST_DILATION * SECTION_FACTOR
    reach = near + far

    shard = conv_weight[0, 0]
    strip = copies_to(shard, "sx", parts_x)
    strip, encode_weight, norm_gain, prior_logits, target_bins, head_weight = lax.optimization_barrier(
        (strip, encode_weight, norm_gain, prior_logits, target_bins, head_weight)
    )
    gain_own = norm_gain[0, 0]
    weights = lax.all_gather(
        strip.reshape(parts_x * shard.shape[0], channels), ("section", "sy"), axis=0, tiled=True
    )
    gain_other = swap(gain_own)
    gain_0 = jnp.where(first, gain_own, gain_other)
    gain_1 = jnp.where(first, gain_other, gain_own)

    blocks = frames[0].reshape(side, 2, side, 2, frames.shape[3])
    kernel = encode_weight.reshape(2, 2, frames.shape[3], channels)
    encoded = jnp.einsum(
        "apbqc,pqco->abo", blocks, kernel, preferred_element_type=jnp.float32
    ).astype(jnp.bfloat16)

    outgoing = jnp.where(first, encoded[side - reach :], encoded[:reach])
    route = [(y, y + 1) for y in range(parts_y - 1)] + [
        (parts_y + y + 1, parts_y + y) for y in range(parts_y - 1)
    ]
    arrived = lax.ppermute(outgoing, ("section", "sy"), route)
    rows = jnp.where(
        first,
        jnp.concatenate([arrived, encoded[: half + reach]], axis=0),
        jnp.concatenate([encoded[half - reach :], arrived], axis=0),
    )
    forward = [(x, x + 1) for x in range(parts_x - 1)]
    backward = [(x + 1, x) for x in range(parts_x - 1)]
    left = lax.ppermute(rows[:, side - reach :], "sx", forward)
    right = lax.ppermute(rows[:, :reach], "sx", backward)
    haloed = jnp.concatenate([left, rows, right], axis=1)

    tall, wide = half + 2 * far, side + 2 * far
    cells = half * side
    stacked = columns_of(norm_gelu(haloed, gain_0), wide, near)
    center = haloed[near : near + tall, near : near + wide]
    prior = lax.dynamic_slice_in_dim(prior_logits[0], section * half, half, axis=0).reshape(cells, bins)
    target = lax.dynamic_slice_in_dim(target_bins[0], section * half, half, axis=0).reshape(cells, 1)
    slots = parts_x * parts_b
    deep = channels * bins // (128 * slots)
    vmem = pl.BlockSpec(memory_space=pltpu.VMEM)
    anywhere = pl.BlockSpec(memory_space=pl.ANY)
    taps = 3 * channels
    own_0, own_1, packed = pl.pallas_call(
        functools.partial(layers_kernel, (far, half, side, 8, slots, parts_y, parts_x)),
        out_shape=(
            jax.ShapeDtypeStruct((half, side, channels), jnp.bfloat16),
            jax.ShapeDtypeStruct((half, side, channels), jnp.bfloat16),
            jax.ShapeDtypeStruct((slots, deep + 8, 128), jnp.bfloat16),
        ),
        in_specs=[anywhere, vmem, anywhere, vmem, vmem, vmem, vmem],
        out_specs=(vmem, vmem, vmem),
        scratch_shapes=[
            pltpu.VMEM((tall + 2 * near, wide, taps), jnp.bfloat16),
            pltpu.VMEM((3 * taps, channels), jnp.bfloat16),
            pltpu.VMEM((3 * taps, channels), jnp.bfloat16),
            pltpu.VMEM((tall, side, taps), jnp.bfloat16),
            pltpu.SemaphoreType.DMA((tall // 8,)),
            pltpu.SemaphoreType.DMA((2,)),
        ],
        compiler_params=pltpu.CompilerParams(vmem_limit_bytes=52 * 2**20),
        cost_estimate=pl.CostEstimate(
            flops=2 * (tall * wide + cells) * 3 * taps * channels,
            bytes_accessed=6 * taps * channels * 2,
            transcendentals=0,
        ),
    )(stacked, center, weights, gain_1.reshape(1, channels), head_weight, prior, target)

    packed = lax.all_to_all(packed, ("sx", "mb"), split_axis=0, concat_axis=0, tiled=True)
    partial = jnp.sum(packed.astype(jnp.float32), axis=0).astype(jnp.bfloat16)
    packed = copies_to(partial, ("section", "sy"), 2 * parts_y)
    partial = jnp.sum(packed.astype(jnp.float32), axis=0)
    loss_all = partial[deep, 0]
    gathered = copies_to(partial[:deep].astype(jnp.bfloat16), ("sx", "mb"), slots)
    scale = lax.rsqrt(jnp.mean(jnp.square(gathered.astype(jnp.float32))) + 1e-06)
    halves = bins // 128
    by_half = gathered.reshape(halves, channels, 128)
    own_rows = lax.dynamic_slice_in_dim(by_half, section * (channels // 2), channels // 2, axis=1)
    head_step = jnp.concatenate(
        [own_rows[h].astype(jnp.float32) * scale for h in range(halves)], axis=1
    )
    mean_loss = loss_all / (parts_b * parts_y * parts_x * side * side)

    sent = swap(jnp.where(first, own_1, own_0))
    grids = jnp.where(
        first, jnp.concatenate([own_0, sent], axis=0), jnp.concatenate([sent, own_1], axis=0)
    )[None, None]
    return (grids, head_step, mean_loss)


def solution(mesh):
    placed = (
        P("mb", "sy", "sx", None),
        P(),
        P("section", None, ("sy", "sx"), None),
        P("section", None, None),
        P(),
        P("mb", "sy", "sx", None),
        P("mb", "sy", "sx"),
    )
    return jax.shard_map(
        per_device,
        mesh=mesh,
        in_specs=placed,
        out_specs=(P("section", "mb", "sy", "sx", None), P("section", None), P()),
        check_vma=False,
    )
```

```python
import functools

import jax
import jax.numpy as jnp
from jax import lax
from jax.experimental import pallas as pl
from jax.experimental.pallas import tpu as pltpu
from jax.sharding import PartitionSpec as P

FIRST_DILATION = 1
SECTION_FACTOR = 8


def norm_gelu(activations, gain):
    values = activations.astype(jnp.float32)
    center = jnp.mean(values, axis=-1, keepdims=True)
    offset = values - center
    spread = jnp.mean(offset * offset, axis=-1, keepdims=True)
    normed = offset * lax.rsqrt(spread + 1e-05) * gain
    return jax.nn.gelu(normed, approximate=False).astype(jnp.bfloat16)


def copies_to(block, axes, count):
    return lax.all_to_all(
        jnp.broadcast_to(block[None], (count,) + block.shape), axes, split_axis=0, concat_axis=0, tiled=True
    )


def swap(block):
    return lax.ppermute(block, "section", [(0, 1), (1, 0)])


def columns_of(padded, wide, step):
    return jnp.concatenate([padded[:, j * step : j * step + wide] for j in range(3)], axis=2)


def erf(value):
    top = 3.832506856900711
    value = jnp.clip(value, -top, top)
    square = value * value
    over = jnp.float32(0.00022905065861350646)
    for term in (0.0034082910107109506, 0.050955695062380861, 0.18520832239976145, 1.128379143519084):
        over = over * square + term
    under = jnp.float32(-1.1791602954361697e-7)
    for term in (
        0.000023547966471313185,
        0.0010179625278914885,
        0.014070470171167667,
        0.11098505178285362,
        0.49746925110067538,
        1.0,
    ):
        under = under * square + term
    return value * over / under


def layers_kernel(
    sizes,
    stacked_hbm,
    center_ref,
    weights_ref,
    gain_ref,
    head_ref,
    prior_ref,
    target_ref,
    out_0_ref,
    out_1_ref,
    packed_ref,
    loss_ref,
    stacked_ref,
    weight_0,
    weight_1,
    hidden_ref,
    gradient_ref,
    sem_s,
    sem_w,
):
    far, half, side, band, slots, parts_y, parts_x = sizes
    tall, wide, taps = stacked_ref.shape[0] - 2, stacked_ref.shape[1], stacked_ref.shape[2]
    channels = taps // 3
    bins = head_ref.shape[1]
    section = lax.axis_index("section")

    def strip(t):
        low = 0 if t == 0 else t * band + 2
        at = pl.ds(low, t * band + band + 2 - low)
        return pltpu.make_async_copy(stacked_hbm.at[at], stacked_ref.at[at], sem_s.at[t])

    strip(0).start()

    def weights(layer, target, sem):
        return pltpu.make_async_copy(weights_ref.at[pl.ds(layer * 3 * taps, 3 * taps)], target, sem)

    fetch_0, fetch_1 = weights(0, weight_0, sem_w.at[0]), weights(1, weight_1, sem_w.at[1])
    fetch_0.start()
    for t in range(1, tall // band):
        strip(t).start()
    fetch_1.start()

    row_start = lax.axis_index("sy") * side + section * half - far
    column_at = lax.axis_index("sx") * side - far + lax.broadcasted_iota(jnp.int32, (band, wide, 1), 1)
    column_in = (column_at >= 0) & (column_at < side * parts_x)
    gain = gain_ref[...].reshape(1, 1, channels)
    fetch_0.wait()
    for t in range(tall // band):
        strip(t).wait()
    for t in range(tall // band):
        total = jnp.dot(
            jnp.concatenate(
                [stacked_ref[t * band + i : t * band + i + band] for i in range(3)], axis=2
            ).reshape(band * wide, 3 * taps),
            weight_0[...],
            preferred_element_type=jnp.float32,
        )
        total = total.reshape(band, wide, channels) + center_ref[t * band : (t + 1) * band].astype(jnp.float32)
        values = total.astype(jnp.bfloat16).astype(jnp.float32)
        if far <= t * band < far + half:
            out_0_ref[t * band - far : (t + 1) * band - far] = values[:, far : far + side].astype(jnp.bfloat16)
        mean = jnp.mean(values, axis=-1, keepdims=True)
        offset = values - mean
        spread = jnp.mean(offset * offset, axis=-1, keepdims=True)
        row_at = row_start + t * band + lax.broadcasted_iota(jnp.int32, (band, wide, 1), 0)
        inside = column_in & (row_at >= 0) & (row_at < side * parts_y)
        normed = offset * jnp.where(inside, lax.rsqrt(spread + 1e-05), 0.0) * gain
        active = 0.5 * normed * (1.0 + erf(normed * 0.7071067811865476))
        for j in range(3):
            hidden_ref[t * band : (t + 1) * band, :, j * channels : (j + 1) * channels] = active[
                :, j * far : j * far + side
            ].astype(jnp.bfloat16)

    cells = half * side
    fetch_1.wait()
    total = jnp.dot(
        jnp.concatenate([hidden_ref[i * far : i * far + half] for i in range(3)], axis=2).reshape(cells, 3 * taps),
        weight_1[...],
        preferred_element_type=jnp.float32,
    )
    flat = (total + out_0_ref[...].reshape(cells, channels).astype(jnp.float32)).astype(jnp.bfloat16)
    out_1_ref[...] = flat.reshape(half, side, channels)
    logits = jnp.dot(flat, head_ref[...], preferred_element_type=jnp.float32)
    logits = logits + prior_ref[...].astype(jnp.float32)
    shifted = logits - jnp.max(logits, axis=1, keepdims=True)
    exp_terms = jnp.exp(shifted)
    exp_total = jnp.sum(exp_terms, axis=1, keepdims=True)
    hit = target_ref[...] == lax.broadcasted_iota(jnp.int32, (cells, bins), 1)
    picked = jnp.sum(jnp.where(hit, shifted, 0.0), axis=1, keepdims=True)
    loss = jnp.sum(jnp.log(exp_total) - picked, axis=0, keepdims=True)
    delta = (exp_terms / exp_total - hit.astype(jnp.float32)).astype(jnp.bfloat16)
    gradient_ref[...] = lax.dot_general(
        flat, delta, (((0,), (0,)), ((), ())), preferred_element_type=jnp.float32
    )
    loss_ref[...] = jnp.broadcast_to(loss, loss_ref.shape)
    piece = packed_ref.shape[1] // 2
    across = channels // (2 * piece)
    for s in range(slots):
        row, lane = (s % across) * piece, (s // across) * 128
        chunk = jnp.concatenate(
            [
                gradient_ref[h * channels // 2 + row : h * channels // 2 + row + piece, lane : lane + 128]
                for h in range(2)
            ],
            axis=0,
        )
        packed_ref[s] = chunk.astype(jnp.bfloat16)


def spread_kernel(arrived_ref, loss_ref, copies_ref):
    total = jnp.sum(arrived_ref[...].astype(jnp.float32), axis=0)
    total = jnp.concatenate([total, loss_ref[...]], axis=0).astype(jnp.bfloat16)
    copies_ref[...] = jnp.broadcast_to(total[None], copies_ref.shape)


def share_kernel(arrived_ref, copies_ref):
    total = jnp.sum(arrived_ref[...].astype(jnp.float32), axis=0)
    deep = total.shape[0] - 8
    piece = deep // 2
    values, loss = total[:deep], total[deep : deep + 1]
    squares = jnp.sum(jnp.sum(values * values, axis=1, keepdims=True), axis=0, keepdims=True)
    squares = jnp.broadcast_to(squares, (1, 128))
    own = jnp.where(lax.axis_index("section") == 0, values[:piece], values[piece:])
    rest = copies_ref.shape[1] - piece
    below = jnp.where(lax.broadcasted_iota(jnp.int32, (rest, 128), 0) == 0, squares, loss)
    block = jnp.concatenate([own, below], axis=0).astype(jnp.bfloat16)
    copies_ref[...] = jnp.broadcast_to(block[None], copies_ref.shape)


def finish_kernel(sizes, arrived_ref, step_ref, loss_ref):
    piece, entries, cells = sizes
    arrived = arrived_ref[...].astype(jnp.float32)
    tails = jnp.sum(arrived, axis=0)
    scale = lax.rsqrt(tails[piece : piece + 1] * (1.0 / entries) + 1e-06)
    loss_ref[...] = tails[piece + 1 : piece + 2] * (1.0 / cells)
    across = step_ref.shape[0] // piece
    for s in range(arrived_ref.shape[0]):
        row, lane = (s % across) * piece, (s // across) * 128
        step_ref[row : row + piece, lane : lane + 128] = arrived[s, :piece] * scale


def per_device(
    frames, encode_weight, conv_weight, norm_gain, head_weight, prior_logits, target_bins
):
    section = lax.axis_index("section")
    first = section == 0
    parts_y = lax.axis_size("sy")
    parts_x = lax.axis_size("sx")
    parts_b = lax.axis_size("mb")
    side = frames.shape[1] // 2
    half = side // 2
    channels = encode_weight.shape[1]
    bins = head_weight.shape[1]
    near = FIRST_DILATION
    far = FIRST_DILATION * SECTION_FACTOR
    reach = near + far

    shard = conv_weight[0, 0]
    strip = copies_to(shard, "sx", parts_x)
    strip, encode_weight, norm_gain, prior_logits, target_bins, head_weight = lax.optimization_barrier(
        (strip, encode_weight, norm_gain, prior_logits, target_bins, head_weight)
    )
    gain_own = norm_gain[0, 0]
    weights = lax.all_gather(
        strip.reshape(parts_x * shard.shape[0], channels), ("section", "sy"), axis=0, tiled=True
    )
    gain_other = swap(gain_own)
    gain_0 = jnp.where(first, gain_own, gain_other)
    gain_1 = jnp.where(first, gain_other, gain_own)

    blocks = frames[0].reshape(side, 2, side, 2, frames.shape[3])
    kernel = encode_weight.reshape(2, 2, frames.shape[3], channels)
    encoded = jnp.einsum(
        "apbqc,pqco->abo", blocks, kernel, preferred_element_type=jnp.float32
    ).astype(jnp.bfloat16)

    outgoing = jnp.where(first, encoded[side - reach :], encoded[:reach])
    route = [(y, y + 1) for y in range(parts_y - 1)] + [
        (parts_y + y + 1, parts_y + y) for y in range(parts_y - 1)
    ]
    arrived = lax.ppermute(outgoing, ("section", "sy"), route)
    rows = jnp.where(
        first,
        jnp.concatenate([arrived, encoded[: half + reach]], axis=0),
        jnp.concatenate([encoded[half - reach :], arrived], axis=0),
    )
    forward = [(x, x + 1) for x in range(parts_x - 1)]
    backward = [(x + 1, x) for x in range(parts_x - 1)]
    left = lax.ppermute(rows[:, side - reach :], "sx", forward)
    right = lax.ppermute(rows[:, :reach], "sx", backward)
    haloed = jnp.concatenate([left, rows, right], axis=1)

    tall, wide = half + 2 * far, side + 2 * far
    cells = half * side
    stacked = columns_of(norm_gelu(haloed, gain_0), wide, near)
    center = haloed[near : near + tall, near : near + wide]
    prior = lax.dynamic_slice_in_dim(prior_logits[0], section * half, half, axis=0).reshape(cells, bins)
    target = lax.dynamic_slice_in_dim(target_bins[0], section * half, half, axis=0).reshape(cells, 1)
    slots = parts_x * parts_b
    deep = channels * bins // (128 * slots)
    vmem = pl.BlockSpec(memory_space=pltpu.VMEM)
    anywhere = pl.BlockSpec(memory_space=pl.ANY)
    taps = 3 * channels
    own_0, own_1, packed, loss = pl.pallas_call(
        functools.partial(layers_kernel, (far, half, side, 8, slots, parts_y, parts_x)),
        out_shape=(
            jax.ShapeDtypeStruct((half, side, channels), jnp.bfloat16),
            jax.ShapeDtypeStruct((half, side, channels), jnp.bfloat16),
            jax.ShapeDtypeStruct((slots, deep, 128), jnp.bfloat16),
            jax.ShapeDtypeStruct((8, 128), jnp.float32),
        ),
        in_specs=[anywhere, vmem, anywhere, vmem, vmem, vmem, vmem],
        out_specs=(vmem, vmem, vmem, vmem),
        scratch_shapes=[
            pltpu.VMEM((tall + 2 * near, wide, taps), jnp.bfloat16),
            pltpu.VMEM((3 * taps, channels), jnp.bfloat16),
            pltpu.VMEM((3 * taps, channels), jnp.bfloat16),
            pltpu.VMEM((tall, side, taps), jnp.bfloat16),
            pltpu.VMEM((channels, bins), jnp.float32),
            pltpu.SemaphoreType.DMA((tall // 8,)),
            pltpu.SemaphoreType.DMA((2,)),
        ],
        compiler_params=pltpu.CompilerParams(vmem_limit_bytes=52 * 2**20),
        cost_estimate=pl.CostEstimate(
            flops=2 * (tall * wide + cells) * 3 * taps * channels,
            bytes_accessed=6 * taps * channels * 2,
            transcendentals=0,
        ),
    )(stacked, center, weights, gain_1.reshape(1, channels), head_weight, prior, target)

    def exchange(blocks, axes):
        return lax.all_to_all(blocks, axes, split_axis=0, concat_axis=0, tiled=True)

    small = pltpu.CompilerParams(vmem_limit_bytes=4 * 2**20)
    packed = exchange(packed, ("sx", "mb"))
    packed = pl.pallas_call(
        spread_kernel, out_shape=jax.ShapeDtypeStruct((2 * parts_y, deep + 8, 128), jnp.bfloat16), compiler_params=small
    )(packed, loss)
    packed = exchange(packed, ("section", "sy"))
    packed = pl.pallas_call(
        share_kernel, out_shape=jax.ShapeDtypeStruct((slots, deep // 2 + 4, 128), jnp.bfloat16), compiler_params=small
    )(packed)
    packed = exchange(packed, ("sx", "mb"))
    head_step, loss = pl.pallas_call(
        functools.partial(
            finish_kernel, (deep // 2, channels * bins, parts_b * parts_y * parts_x * side * side)
        ),
        out_shape=(
            jax.ShapeDtypeStruct((channels // 2, bins), jnp.float32),
            jax.ShapeDtypeStruct((1, 128), jnp.float32),
        ),
        compiler_params=small,
    )(packed)
    mean_loss = loss[0, 0]

    sent = swap(jnp.where(first, own_1, own_0))
    grids = jnp.where(
        first, jnp.concatenate([own_0, sent], axis=0), jnp.concatenate([sent, own_1], axis=0)
    )[None, None]
    return (grids, head_step, mean_loss)


def solution(mesh):
    placed = (
        P("mb", "sy", "sx", None),
        P(),
        P("section", None, ("sy", "sx"), None),
        P("section", None, None),
        P(),
        P("mb", "sy", "sx", None),
        P("mb", "sy", "sx"),
    )
    return jax.shard_map(
        per_device,
        mesh=mesh,
        in_specs=placed,
        out_specs=(P("section", "mb", "sy", "sx", None), P("section", None), P()),
        check_vma=False,
    )
```

```python
import functools

import jax
import jax.numpy as jnp
from jax import lax
from jax.experimental import pallas as pl
from jax.experimental.pallas import tpu as pltpu
from jax.sharding import PartitionSpec as P

FIRST_DILATION = 1
SECTION_FACTOR = 8


def copies_to(block, axes, count):
    return lax.all_to_all(
        jnp.broadcast_to(block[None], (count,) + block.shape), axes, split_axis=0, concat_axis=0, tiled=True
    )


def swap(block):
    return lax.ppermute(block, "section", [(0, 1), (1, 0)])


def erf(value):
    top = 3.832506856900711
    value = jnp.clip(value, -top, top)
    square = value * value
    over = jnp.float32(0.00022905065861350646)
    for term in (0.0034082910107109506, 0.050955695062380861, 0.18520832239976145, 1.128379143519084):
        over = over * square + term
    under = jnp.float32(-1.1791602954361697e-7)
    for term in (
        0.000023547966471313185,
        0.0010179625278914885,
        0.014070470171167667,
        0.11098505178285362,
        0.49746925110067538,
        1.0,
    ):
        under = under * square + term
    return value * over / under


def layers_kernel(
    sizes,
    stacked_hbm,
    center_hbm,
    weights_ref,
    gain_ref,
    head_ref,
    prior_ref,
    target_ref,
    out_0_ref,
    out_1_ref,
    packed_ref,
    loss_ref,
    stacked_ref,
    center_ref,
    weight_0,
    weight_1,
    hidden_ref,
    sem_s,
    sem_w,
):
    far, half, side, band, slots, parts_y, parts_x = sizes
    tall, wide, taps = stacked_ref.shape[0] - 2, stacked_ref.shape[1], stacked_ref.shape[2]
    channels = taps // 3
    bins = head_ref.shape[1]
    section = lax.axis_index("section")

    def strip(t):
        low = 0 if t == 0 else t * band + 2
        at = pl.ds(low, t * band + band + 2 - low)
        return pltpu.make_async_copy(stacked_hbm.at[at], stacked_ref.at[at], sem_s.at[t])

    strip(0).start()

    def weights(layer, target, sem):
        return pltpu.make_async_copy(weights_ref.at[pl.ds(layer * 3 * taps, 3 * taps)], target, sem)

    fetch_0, fetch_1 = weights(0, weight_0, sem_w.at[0]), weights(1, weight_1, sem_w.at[1])
    fetch_0.start()
    for t in range(1, tall // band):
        strip(t).start()
    fetch_center = pltpu.make_async_copy(center_hbm, center_ref, sem_w.at[2])
    fetch_center.start()
    fetch_1.start()

    row_start = lax.axis_index("sy") * side + section * half - far
    column_at = lax.axis_index("sx") * side - far + lax.broadcasted_iota(jnp.int32, (band, wide, 1), 1)
    column_in = (column_at >= 0) & (column_at < side * parts_x)
    gain = gain_ref[...].reshape(1, 1, channels)
    fetch_0.wait()
    for t in range(tall // band):
        strip(t).wait()
    for t in range(tall // band):
        total = jnp.dot(
            jnp.concatenate(
                [stacked_ref[t * band + i : t * band + i + band] for i in range(3)], axis=2
            ).reshape(band * wide, 3 * taps),
            weight_0[...],
            preferred_element_type=jnp.float32,
        )
        if t == 0:
            fetch_center.wait()
        total = total.reshape(band, wide, channels) + center_ref[t * band : (t + 1) * band].astype(jnp.float32)
        values = total.astype(jnp.bfloat16).astype(jnp.float32)
        if far <= t * band < far + half:
            out_0_ref[t * band - far : (t + 1) * band - far] = values[:, far : far + side].astype(jnp.bfloat16)
        mean = jnp.mean(values, axis=-1, keepdims=True)
        offset = values - mean
        spread = jnp.mean(offset * offset, axis=-1, keepdims=True)
        row_at = row_start + t * band + lax.broadcasted_iota(jnp.int32, (band, wide, 1), 0)
        inside = column_in & (row_at >= 0) & (row_at < side * parts_y)
        normed = offset * jnp.where(inside, lax.rsqrt(spread + 1e-05), 0.0) * gain
        active = 0.5 * normed * (1.0 + erf(normed * 0.7071067811865476))
        for j in range(3):
            hidden_ref[t * band : (t + 1) * band, :, j * channels : (j + 1) * channels] = active[
                :, j * far : j * far + side
            ].astype(jnp.bfloat16)

    cells = half * side
    fetch_1.wait()
    total = jnp.dot(
        jnp.concatenate([hidden_ref[i * far : i * far + half] for i in range(3)], axis=2).reshape(cells, 3 * taps),
        weight_1[...],
        preferred_element_type=jnp.float32,
    )
    flat = (total + out_0_ref[...].reshape(cells, channels).astype(jnp.float32)).astype(jnp.bfloat16)
    out_1_ref[...] = flat.reshape(half, side, channels)
    logits = jnp.dot(flat, head_ref[...], preferred_element_type=jnp.float32)
    logits = logits + prior_ref[...].astype(jnp.float32)
    shifted = logits - jnp.max(logits, axis=1, keepdims=True)
    exp_terms = jnp.exp(shifted)
    exp_total = jnp.sum(exp_terms, axis=1, keepdims=True)
    hit = target_ref[...] == lax.broadcasted_iota(jnp.int32, (cells, bins), 1)
    picked = jnp.sum(jnp.where(hit, shifted, 0.0), axis=1, keepdims=True)
    loss = jnp.sum(jnp.log(exp_total) - picked, axis=0, keepdims=True)
    delta = (exp_terms / exp_total - hit.astype(jnp.float32)).astype(jnp.bfloat16)
    gradient = lax.dot_general(
        flat, delta, (((0,), (0,)), ((), ())), preferred_element_type=jnp.float32
    )
    loss_ref[...] = jnp.broadcast_to(loss, loss_ref.shape)
    deep = packed_ref.shape[1]
    middle = channels // 2
    across = middle // deep
    left = lax.broadcasted_iota(jnp.int32, (middle, 128), 1) < 64
    for q in range(bins // 128):
        upper = gradient[:middle, q * 128 : (q + 1) * 128]
        lower = gradient[middle:, q * 128 : (q + 1) * 128]
        pair = (
            jnp.where(left, upper, pltpu.roll(lower, 64, 1)),
            jnp.where(left, pltpu.roll(upper, 64, 1), lower),
        )
        for p in range(2):
            for r in range(across):
                packed_ref[(2 * q + p) * across + r] = pair[p][r * deep : (r + 1) * deep].astype(jnp.bfloat16)


def spread_kernel(arrived_ref, loss_ref, copies_ref):
    total = jnp.sum(arrived_ref[...].astype(jnp.float32), axis=0)
    total = jnp.concatenate([total, loss_ref[...]], axis=0).astype(jnp.bfloat16)
    copies_ref[...] = jnp.broadcast_to(total[None], copies_ref.shape)


def share_kernel(arrived_ref, copies_ref):
    total = jnp.sum(arrived_ref[...].astype(jnp.float32), axis=0)
    deep = total.shape[0] - 8
    values, loss = total[:deep], total[deep : deep + 8]
    squares = jnp.sum(jnp.sum(values * values, axis=1, keepdims=True), axis=0, keepdims=True)
    turned = pltpu.roll(values, 64, 1)
    first = lax.axis_index("section") == 0
    own_left = jnp.where(first, values, turned)
    own_right = jnp.where(first, turned, values)
    tail = jnp.where(lax.broadcasted_iota(jnp.int32, (8, 128), 0) == 0, squares, loss)
    left = lax.broadcasted_iota(jnp.int32, (16, 128), 1) < 64
    block = jnp.where(left, own_left[:16], jnp.concatenate([own_right[16:deep], tail], axis=0))
    copies_ref[...] = jnp.broadcast_to(block.astype(jnp.bfloat16)[None], copies_ref.shape)


def finish_kernel(sizes, arrived_ref, step_ref, loss_ref):
    entries, cells = sizes
    arrived = arrived_ref[...].astype(jnp.float32)
    tails = jnp.sum(arrived[:, 8:], axis=0)
    scale = lax.rsqrt(tails[0:1, 127:128] * (1.0 / entries) + 1e-06)
    loss_ref[...] = jnp.broadcast_to(tails[1:2, 127:128] * (1.0 / cells), loss_ref.shape)
    deep = 24
    across = step_ref.shape[0] // deep
    left = lax.broadcasted_iota(jnp.int32, (deep, 128), 1) < 64

    def piece(s):
        block = arrived[s]
        return jnp.concatenate([block, pltpu.roll(block[:8], 64, 1)], axis=0)

    for q in range(step_ref.shape[1] // 128):
        for r in range(across):
            right = pltpu.roll(piece((2 * q + 1) * across + r), 64, 1)
            both = jnp.where(left, piece(2 * q * across + r), right) * scale
            step_ref[r * deep : (r + 1) * deep, q * 128 : (q + 1) * 128] = both


def window_kernel(sizes, left_ref, rows_ref, right_ref, gain_ref, stacked_ref, center_ref, grid_ref, active_ref):
    near, band = sizes
    rows, side, channels = rows_ref.shape
    reach = left_ref.shape[1]
    wide = side + 2 * (reach - near)
    grid_ref[...] = jnp.zeros(grid_ref.shape, jnp.float32)
    grid_ref[:, :reach] = left_ref[...].astype(jnp.float32)
    grid_ref[:, reach : reach + side] = rows_ref[...].astype(jnp.float32)
    grid_ref[:, reach + side : 2 * reach + side] = right_ref[...].astype(jnp.float32)
    gain = gain_ref[...].reshape(1, 1, channels)
    for t in range(rows // band):
        at = slice(t * band, (t + 1) * band)
        values = grid_ref[at]
        offset = values - jnp.mean(values, axis=-1, keepdims=True)
        spread = jnp.mean(offset * offset, axis=-1, keepdims=True)
        normed = offset * lax.rsqrt(spread + 1e-05) * gain
        active_ref[...] = 0.5 * normed * (1.0 + erf(normed * 0.7071067811865476))
        for j in range(3):
            stacked_ref[at, :, j * channels : (j + 1) * channels] = active_ref[
                :, j * near : j * near + wide
            ].astype(jnp.bfloat16)
    center_ref[...] = grid_ref[near : rows - near, near : near + wide].astype(jnp.bfloat16)


def per_device(
    frames, encode_weight, conv_weight, norm_gain, head_weight, prior_logits, target_bins
):
    section = lax.axis_index("section")
    first = section == 0
    parts_y = lax.axis_size("sy")
    parts_x = lax.axis_size("sx")
    parts_b = lax.axis_size("mb")
    side = frames.shape[1] // 2
    half = side // 2
    channels = encode_weight.shape[1]
    bins = head_weight.shape[1]
    near = FIRST_DILATION
    far = FIRST_DILATION * SECTION_FACTOR
    reach = near + far

    shard = conv_weight[0, 0]
    strip = copies_to(shard, "sx", parts_x)
    strip, encode_weight, norm_gain, prior_logits, target_bins, head_weight = lax.optimization_barrier(
        (strip, encode_weight, norm_gain, prior_logits, target_bins, head_weight)
    )
    gain_own = norm_gain[0, 0]
    weights = lax.all_gather(
        strip.reshape(parts_x * shard.shape[0], channels), ("section", "sy"), axis=0, tiled=True
    )
    gain_other = swap(gain_own)
    gain_0 = jnp.where(first, gain_own, gain_other)
    gain_1 = jnp.where(first, gain_other, gain_own)

    blocks = frames[0].reshape(side, 2, side, 2, frames.shape[3])
    kernel = encode_weight.reshape(2, 2, frames.shape[3], channels)
    encoded = jnp.einsum(
        "apbqc,pqco->abo", blocks, kernel, preferred_element_type=jnp.float32
    ).astype(jnp.bfloat16)

    outgoing = jnp.where(first, encoded[side - reach :], encoded[:reach])
    route = [(y, y + 1) for y in range(parts_y - 1)] + [
        (parts_y + y + 1, parts_y + y) for y in range(parts_y - 1)
    ]
    arrived = lax.ppermute(outgoing, ("section", "sy"), route)
    rows = jnp.where(
        first,
        jnp.concatenate([arrived, encoded[: half + reach]], axis=0),
        jnp.concatenate([encoded[half - reach :], arrived], axis=0),
    )
    forward = [(x, x + 1) for x in range(parts_x - 1)]
    backward = [(x + 1, x) for x in range(parts_x - 1)]
    left = lax.ppermute(rows[:, side - reach :], "sx", forward)
    right = lax.ppermute(rows[:, :reach], "sx", backward)

    tall, wide = half + 2 * far, side + 2 * far
    cells = half * side
    columns = -(-(side + 2 * reach) // 8) * 8
    stacked, center = pl.pallas_call(
        functools.partial(window_kernel, (near, 2)),
        out_shape=(
            jax.ShapeDtypeStruct((tall + 2 * near, wide, 3 * channels), jnp.bfloat16),
            jax.ShapeDtypeStruct((tall, wide, channels), jnp.bfloat16),
        ),
        scratch_shapes=[
            pltpu.VMEM((tall + 2 * near, columns, channels), jnp.float32),
            pltpu.VMEM((2, columns, channels), jnp.float32),
        ],
        compiler_params=pltpu.CompilerParams(vmem_limit_bytes=32 * 2**20),
    )(left, rows, right, gain_0.reshape(1, channels))
    prior = lax.dynamic_slice_in_dim(prior_logits[0], section * half, half, axis=0).reshape(cells, bins)
    target = lax.dynamic_slice_in_dim(target_bins[0], section * half, half, axis=0).reshape(cells, 1)
    slots = parts_x * parts_b
    deep = channels * bins // (128 * slots)
    vmem = pl.BlockSpec(memory_space=pltpu.VMEM)
    anywhere = pl.BlockSpec(memory_space=pl.ANY)
    taps = 3 * channels
    own_0, own_1, packed, loss = pl.pallas_call(
        functools.partial(layers_kernel, (far, half, side, 8, slots, parts_y, parts_x)),
        out_shape=(
            jax.ShapeDtypeStruct((half, side, channels), jnp.bfloat16),
            jax.ShapeDtypeStruct((half, side, channels), jnp.bfloat16),
            jax.ShapeDtypeStruct((slots, deep, 128), jnp.bfloat16),
            jax.ShapeDtypeStruct((8, 128), jnp.float32),
        ),
        in_specs=[anywhere, anywhere, anywhere, vmem, vmem, vmem, vmem],
        out_specs=(vmem, vmem, vmem, vmem),
        scratch_shapes=[
            pltpu.VMEM((tall + 2 * near, wide, taps), jnp.bfloat16),
            pltpu.VMEM((tall, wide, channels), jnp.bfloat16),
            pltpu.VMEM((3 * taps, channels), jnp.bfloat16),
            pltpu.VMEM((3 * taps, channels), jnp.bfloat16),
            pltpu.VMEM((tall, side, taps), jnp.bfloat16),
            pltpu.SemaphoreType.DMA((tall // 8,)),
            pltpu.SemaphoreType.DMA((3,)),
        ],
        compiler_params=pltpu.CompilerParams(vmem_limit_bytes=52 * 2**20),
        cost_estimate=pl.CostEstimate(
            flops=2 * (tall * wide + cells) * 3 * taps * channels,
            bytes_accessed=6 * taps * channels * 2,
            transcendentals=0,
        ),
    )(stacked, center, weights, gain_1.reshape(1, channels), head_weight, prior, target)

    def exchange(blocks, axes):
        return lax.all_to_all(blocks, axes, split_axis=0, concat_axis=0, tiled=True)

    small = pltpu.CompilerParams(vmem_limit_bytes=4 * 2**20)
    packed = exchange(packed, ("sx", "mb"))
    packed = pl.pallas_call(
        spread_kernel, out_shape=jax.ShapeDtypeStruct((2 * parts_y, deep + 8, 128), jnp.bfloat16), compiler_params=small
    )(packed, loss)
    packed = exchange(packed, ("section", "sy"))
    packed = pl.pallas_call(
        share_kernel, out_shape=jax.ShapeDtypeStruct((slots, 16, 128), jnp.bfloat16), compiler_params=small
    )(packed)
    packed = exchange(packed, ("sx", "mb"))
    head_step, loss = pl.pallas_call(
        functools.partial(
            finish_kernel, (channels * bins, parts_b * parts_y * parts_x * side * side)
        ),
        out_shape=(
            jax.ShapeDtypeStruct((channels // 2, bins), jnp.float32),
            jax.ShapeDtypeStruct((1, 128), jnp.float32),
        ),
        compiler_params=small,
    )(packed)
    mean_loss = loss[0, 0]

    sent = swap(jnp.where(first, own_1, own_0))
    grids = jnp.where(
        first, jnp.concatenate([own_0, sent], axis=0), jnp.concatenate([sent, own_1], axis=0)
    )[None, None]
    return (grids, head_step, mean_loss)


def solution(mesh):
    placed = (
        P("mb", "sy", "sx", None),
        P(),
        P("section", None, ("sy", "sx"), None),
        P("section", None, None),
        P(),
        P("mb", "sy", "sx", None),
        P("mb", "sy", "sx"),
    )
    return jax.shard_map(
        per_device,
        mesh=mesh,
        in_specs=placed,
        out_specs=(P("section", "mb", "sy", "sx", None), P("section", None), P()),
        check_vma=False,
    )
```

```python
import functools

import jax
import jax.numpy as jnp
from jax import lax
from jax.experimental import pallas as pl
from jax.experimental.pallas import tpu as pltpu
from jax.sharding import PartitionSpec as P

FIRST_DILATION = 1
SECTION_FACTOR = 8


def copies_to(block, axes, count):
    return lax.all_to_all(
        jnp.broadcast_to(block[None], (count,) + block.shape), axes, split_axis=0, concat_axis=0, tiled=True
    )


def swap(block):
    return lax.ppermute(block, "section", [(0, 1), (1, 0)])


def erf(value):
    top = 3.832506856900711
    value = jnp.clip(value, -top, top)
    square = value * value
    over = jnp.float32(0.00022905065861350646)
    for term in (0.0034082910107109506, 0.050955695062380861, 0.18520832239976145, 1.128379143519084):
        over = over * square + term
    under = jnp.float32(-1.1791602954361697e-7)
    for term in (
        0.000023547966471313185,
        0.0010179625278914885,
        0.014070470171167667,
        0.11098505178285362,
        0.49746925110067538,
        1.0,
    ):
        under = under * square + term
    return value * over / under


def layers_kernel(
    sizes,
    stacked_hbm,
    center_hbm,
    weights_ref,
    gain_ref,
    head_ref,
    prior_ref,
    target_ref,
    out_0_ref,
    out_1_ref,
    packed_ref,
    loss_ref,
    stacked_ref,
    center_ref,
    weight_0,
    weight_1,
    hidden_ref,
    sem_s,
    sem_w,
):
    far, half, side, band, slots, parts_y, parts_x = sizes
    tall, wide, taps = stacked_ref.shape[0] - 2, stacked_ref.shape[1], stacked_ref.shape[2]
    channels = taps // 3
    bins = head_ref.shape[1]
    section = lax.axis_index("section")

    def strip(t):
        low = 0 if t == 0 else t * band + 2
        at = pl.ds(low, t * band + band + 2 - low)
        return pltpu.make_async_copy(stacked_hbm.at[at], stacked_ref.at[at], sem_s.at[t])

    strip(0).start()

    def third(i):
        at = pl.ds(i * taps, taps)
        return pltpu.make_async_copy(weights_ref.at[at], weight_0.at[at], sem_w.at[i])

    fetch_1 = pltpu.make_async_copy(weights_ref.at[pl.ds(3 * taps, 3 * taps)], weight_1, sem_w.at[3])
    for i in range(3):
        third(i).start()
    for t in range(1, tall // band):
        strip(t).start()
    fetch_center = pltpu.make_async_copy(center_hbm, center_ref, sem_w.at[4])
    fetch_center.start()
    fetch_1.start()

    row_start = lax.axis_index("sy") * side + section * half - far
    column_at = lax.axis_index("sx") * side - far + lax.broadcasted_iota(jnp.int32, (band, wide, 1), 1)
    column_in = (column_at >= 0) & (column_at < side * parts_x)
    gain = gain_ref[...].reshape(1, 1, channels)
    strip(0).wait()
    start = jnp.zeros((band * wide, channels), jnp.float32)
    for i in range(3):
        third(i).wait()
        start += jnp.dot(
            stacked_ref[i : i + band].reshape(band * wide, taps),
            weight_0[i * taps : (i + 1) * taps],
            preferred_element_type=jnp.float32,
        )
    for t in range(1, tall // band):
        strip(t).wait()
    fetch_center.wait()
    for t in range(tall // band):
        total = start if t == 0 else jnp.dot(
            jnp.concatenate(
                [stacked_ref[t * band + i : t * band + i + band] for i in range(3)], axis=2
            ).reshape(band * wide, 3 * taps),
            weight_0[...],
            preferred_element_type=jnp.float32,
        )
        total = total.reshape(band, wide, channels) + center_ref[t * band : (t + 1) * band].astype(jnp.float32)
        values = total.astype(jnp.bfloat16).astype(jnp.float32)
        if far <= t * band < far + half:
            out_0_ref[t * band - far : (t + 1) * band - far] = values[:, far : far + side].astype(jnp.bfloat16)
        mean = jnp.mean(values, axis=-1, keepdims=True)
        offset = values - mean
        spread = jnp.mean(offset * offset, axis=-1, keepdims=True)
        row_at = row_start + t * band + lax.broadcasted_iota(jnp.int32, (band, wide, 1), 0)
        inside = column_in & (row_at >= 0) & (row_at < side * parts_y)
        normed = offset * jnp.where(inside, lax.rsqrt(spread + 1e-05), 0.0) * gain
        active = 0.5 * normed * (1.0 + erf(normed * 0.7071067811865476))
        for j in range(3):
            hidden_ref[t * band : (t + 1) * band, :, j * channels : (j + 1) * channels] = active[
                :, j * far : j * far + side
            ].astype(jnp.bfloat16)

    cells = half * side
    fetch_1.wait()
    total = jnp.dot(
        jnp.concatenate([hidden_ref[i * far : i * far + half] for i in range(3)], axis=2).reshape(cells, 3 * taps),
        weight_1[...],
        preferred_element_type=jnp.float32,
    )
    flat = (total + out_0_ref[...].reshape(cells, channels).astype(jnp.float32)).astype(jnp.bfloat16)
    out_1_ref[...] = flat.reshape(half, side, channels)
    logits = jnp.dot(flat, head_ref[...], preferred_element_type=jnp.float32)
    logits = logits + prior_ref[...].astype(jnp.float32)
    shifted = logits - jnp.max(logits, axis=1, keepdims=True)
    exp_terms = jnp.exp(shifted)
    exp_total = jnp.sum(exp_terms, axis=1, keepdims=True)
    hit = target_ref[...] == lax.broadcasted_iota(jnp.int32, (cells, bins), 1)
    picked = jnp.sum(jnp.where(hit, shifted, 0.0), axis=1, keepdims=True)
    loss = jnp.sum(jnp.log(exp_total) - picked, axis=0, keepdims=True)
    delta = (exp_terms / exp_total - hit.astype(jnp.float32)).astype(jnp.bfloat16)
    gradient = lax.dot_general(
        flat, delta, (((0,), (0,)), ((), ())), preferred_element_type=jnp.float32
    )
    loss_ref[...] = jnp.broadcast_to(loss, loss_ref.shape)
    deep = packed_ref.shape[1]
    middle = channels // 2
    across = middle // deep
    left = lax.broadcasted_iota(jnp.int32, (middle, 128), 1) < 64
    for q in range(bins // 128):
        upper = gradient[:middle, q * 128 : (q + 1) * 128]
        lower = gradient[middle:, q * 128 : (q + 1) * 128]
        pair = (
            jnp.where(left, upper, pltpu.roll(lower, 64, 1)),
            jnp.where(left, pltpu.roll(upper, 64, 1), lower),
        )
        for p in range(2):
            for r in range(across):
                packed_ref[(2 * q + p) * across + r] = pair[p][r * deep : (r + 1) * deep].astype(jnp.bfloat16)


def spread_kernel(arrived_ref, loss_ref, copies_ref):
    total = jnp.sum(arrived_ref[...].astype(jnp.float32), axis=0)
    total = jnp.concatenate([total, loss_ref[...]], axis=0).astype(jnp.bfloat16)
    copies_ref[...] = jnp.broadcast_to(total[None], copies_ref.shape)


def share_kernel(arrived_ref, copies_ref):
    total = jnp.sum(arrived_ref[...].astype(jnp.float32), axis=0)
    deep = total.shape[0] - 8
    values, loss = total[:deep], total[deep : deep + 8]
    squares = jnp.sum(jnp.sum(values * values, axis=1, keepdims=True), axis=0, keepdims=True)
    turned = pltpu.roll(values, 64, 1)
    first = lax.axis_index("section") == 0
    own_left = jnp.where(first, values, turned)
    own_right = jnp.where(first, turned, values)
    tail = jnp.where(lax.broadcasted_iota(jnp.int32, (8, 128), 0) == 0, squares, loss)
    left = lax.broadcasted_iota(jnp.int32, (16, 128), 1) < 64
    block = jnp.where(left, own_left[:16], jnp.concatenate([own_right[16:deep], tail], axis=0))
    copies_ref[...] = jnp.broadcast_to(block.astype(jnp.bfloat16)[None], copies_ref.shape)


def finish_kernel(sizes, arrived_ref, step_ref, loss_ref):
    entries, cells = sizes
    arrived = arrived_ref[...].astype(jnp.float32)
    tails = jnp.sum(arrived[:, 8:], axis=0)
    scale = lax.rsqrt(tails[0:1, 127:128] * (1.0 / entries) + 1e-06)
    loss_ref[...] = jnp.broadcast_to(tails[1:2, 127:128] * (1.0 / cells), loss_ref.shape)
    deep = 24
    across = step_ref.shape[0] // deep
    left = lax.broadcasted_iota(jnp.int32, (deep, 128), 1) < 64

    def piece(s):
        block = arrived[s]
        return jnp.concatenate([block, pltpu.roll(block[:8], 64, 1)], axis=0)

    for q in range(step_ref.shape[1] // 128):
        for r in range(across):
            right = pltpu.roll(piece((2 * q + 1) * across + r), 64, 1)
            both = jnp.where(left, piece(2 * q * across + r), right) * scale
            step_ref[r * deep : (r + 1) * deep, q * 128 : (q + 1) * 128] = both


def window_kernel(sizes, left_ref, rows_ref, right_ref, gain_ref, stacked_ref, center_ref, grid_ref, active_ref):
    near, band = sizes
    rows, side, channels = rows_ref.shape
    reach = left_ref.shape[1]
    wide = side + 2 * (reach - near)
    grid_ref[...] = jnp.zeros(grid_ref.shape, jnp.float32)
    grid_ref[:, :reach] = left_ref[...].astype(jnp.float32)
    grid_ref[:, reach : reach + side] = rows_ref[...].astype(jnp.float32)
    grid_ref[:, reach + side : 2 * reach + side] = right_ref[...].astype(jnp.float32)
    gain = gain_ref[...].reshape(1, 1, channels)
    for t in range(rows // band):
        at = slice(t * band, (t + 1) * band)
        values = grid_ref[at]
        offset = values - jnp.mean(values, axis=-1, keepdims=True)
        spread = jnp.mean(offset * offset, axis=-1, keepdims=True)
        normed = offset * lax.rsqrt(spread + 1e-05) * gain
        active_ref[...] = 0.5 * normed * (1.0 + erf(normed * 0.7071067811865476))
        for j in range(3):
            stacked_ref[at, :, j * channels : (j + 1) * channels] = active_ref[
                :, j * near : j * near + wide
            ].astype(jnp.bfloat16)
    center_ref[...] = grid_ref[near : rows - near, near : near + wide].astype(jnp.bfloat16)


def per_device(
    frames, encode_weight, conv_weight, norm_gain, head_weight, prior_logits, target_bins
):
    section = lax.axis_index("section")
    first = section == 0
    parts_y = lax.axis_size("sy")
    parts_x = lax.axis_size("sx")
    parts_b = lax.axis_size("mb")
    side = frames.shape[1] // 2
    half = side // 2
    channels = encode_weight.shape[1]
    bins = head_weight.shape[1]
    near = FIRST_DILATION
    far = FIRST_DILATION * SECTION_FACTOR
    reach = near + far

    shard = conv_weight[0, 0]
    strip = copies_to(shard, "sx", parts_x)
    strip, encode_weight, norm_gain, prior_logits, target_bins, head_weight = lax.optimization_barrier(
        (strip, encode_weight, norm_gain, prior_logits, target_bins, head_weight)
    )
    gain_own = norm_gain[0, 0]
    weights = lax.all_gather(
        strip.reshape(parts_x * shard.shape[0], channels), ("section", "sy"), axis=0, tiled=True
    )
    gain_other = swap(gain_own)
    gain_0 = jnp.where(first, gain_own, gain_other)
    gain_1 = jnp.where(first, gain_other, gain_own)

    blocks = frames[0].reshape(side, 2, side, 2, frames.shape[3])
    kernel = encode_weight.reshape(2, 2, frames.shape[3], channels)
    encoded = jnp.einsum(
        "apbqc,pqco->abo", blocks, kernel, preferred_element_type=jnp.float32
    ).astype(jnp.bfloat16)

    outgoing = jnp.where(first, encoded[side - reach :], encoded[:reach])
    route = [(y, y + 1) for y in range(parts_y - 1)] + [
        (parts_y + y + 1, parts_y + y) for y in range(parts_y - 1)
    ]
    arrived = lax.ppermute(outgoing, ("section", "sy"), route)
    rows = jnp.where(
        first,
        jnp.concatenate([arrived, encoded[: half + reach]], axis=0),
        jnp.concatenate([encoded[half - reach :], arrived], axis=0),
    )
    forward = [(x, x + 1) for x in range(parts_x - 1)]
    backward = [(x + 1, x) for x in range(parts_x - 1)]
    left = lax.ppermute(rows[:, side - reach :], "sx", forward)
    right = lax.ppermute(rows[:, :reach], "sx", backward)

    tall, wide = half + 2 * far, side + 2 * far
    cells = half * side
    columns = -(-(side + 2 * reach) // 8) * 8
    stacked, center = pl.pallas_call(
        functools.partial(window_kernel, (near, 2)),
        out_shape=(
            jax.ShapeDtypeStruct((tall + 2 * near, wide, 3 * channels), jnp.bfloat16),
            jax.ShapeDtypeStruct((tall, wide, channels), jnp.bfloat16),
        ),
        scratch_shapes=[
            pltpu.VMEM((tall + 2 * near, columns, channels), jnp.float32),
            pltpu.VMEM((2, columns, channels), jnp.float32),
        ],
        compiler_params=pltpu.CompilerParams(vmem_limit_bytes=32 * 2**20),
    )(left, rows, right, gain_0.reshape(1, channels))
    prior = lax.dynamic_slice_in_dim(prior_logits[0], section * half, half, axis=0).reshape(cells, bins)
    target = lax.dynamic_slice_in_dim(target_bins[0], section * half, half, axis=0).reshape(cells, 1)
    slots = parts_x * parts_b
    deep = channels * bins // (128 * slots)
    vmem = pl.BlockSpec(memory_space=pltpu.VMEM)
    anywhere = pl.BlockSpec(memory_space=pl.ANY)
    taps = 3 * channels
    own_0, own_1, packed, loss = pl.pallas_call(
        functools.partial(layers_kernel, (far, half, side, 8, slots, parts_y, parts_x)),
        out_shape=(
            jax.ShapeDtypeStruct((half, side, channels), jnp.bfloat16),
            jax.ShapeDtypeStruct((half, side, channels), jnp.bfloat16),
            jax.ShapeDtypeStruct((slots, deep, 128), jnp.bfloat16),
            jax.ShapeDtypeStruct((8, 128), jnp.float32),
        ),
        in_specs=[anywhere, anywhere, anywhere, vmem, vmem, vmem, vmem],
        out_specs=(vmem, vmem, vmem, vmem),
        scratch_shapes=[
            pltpu.VMEM((tall + 2 * near, wide, taps), jnp.bfloat16),
            pltpu.VMEM((tall, wide, channels), jnp.bfloat16),
            pltpu.VMEM((3 * taps, channels), jnp.bfloat16),
            pltpu.VMEM((3 * taps, channels), jnp.bfloat16),
            pltpu.VMEM((tall, side, taps), jnp.bfloat16),
            pltpu.SemaphoreType.DMA((tall // 8,)),
            pltpu.SemaphoreType.DMA((5,)),
        ],
        compiler_params=pltpu.CompilerParams(vmem_limit_bytes=52 * 2**20),
        cost_estimate=pl.CostEstimate(
            flops=2 * (tall * wide + cells) * 3 * taps * channels,
            bytes_accessed=6 * taps * channels * 2,
            transcendentals=0,
        ),
    )(stacked, center, weights, gain_1.reshape(1, channels), head_weight, prior, target)

    def exchange(blocks, axes):
        return lax.all_to_all(blocks, axes, split_axis=0, concat_axis=0, tiled=True)

    small = pltpu.CompilerParams(vmem_limit_bytes=4 * 2**20)
    packed = exchange(packed, ("sx", "mb"))
    packed = pl.pallas_call(
        spread_kernel, out_shape=jax.ShapeDtypeStruct((2 * parts_y, deep + 8, 128), jnp.bfloat16), compiler_params=small
    )(packed, loss)
    packed = exchange(packed, ("section", "sy"))
    packed = pl.pallas_call(
        share_kernel, out_shape=jax.ShapeDtypeStruct((slots, 16, 128), jnp.bfloat16), compiler_params=small
    )(packed)
    packed = exchange(packed, ("sx", "mb"))
    head_step, loss = pl.pallas_call(
        functools.partial(
            finish_kernel, (channels * bins, parts_b * parts_y * parts_x * side * side)
        ),
        out_shape=(
            jax.ShapeDtypeStruct((channels // 2, bins), jnp.float32),
            jax.ShapeDtypeStruct((1, 128), jnp.float32),
        ),
        compiler_params=small,
    )(packed)
    mean_loss = loss[0, 0]

    sent = swap(jnp.where(first, own_1, own_0))
    grids = jnp.where(
        first, jnp.concatenate([own_0, sent], axis=0), jnp.concatenate([sent, own_1], axis=0)
    )[None, None]
    return (grids, head_step, mean_loss)


def solution(mesh):
    placed = (
        P("mb", "sy", "sx", None),
        P(),
        P("section", None, ("sy", "sx"), None),
        P("section", None, None),
        P(),
        P("mb", "sy", "sx", None),
        P("mb", "sy", "sx"),
    )
    return jax.shard_map(
        per_device,
        mesh=mesh,
        in_specs=placed,
        out_specs=(P("section", "mb", "sy", "sx", None), P("section", None), P()),
        check_vma=False,
    )
```

```python
import functools

import jax
import jax.numpy as jnp
from jax import lax
from jax.experimental import pallas as pl
from jax.experimental.pallas import tpu as pltpu
from jax.sharding import PartitionSpec as P

FIRST_DILATION = 1
SECTION_FACTOR = 8


def copies_to(block, axes, count):
    return lax.all_to_all(
        jnp.broadcast_to(block[None], (count,) + block.shape), axes, split_axis=0, concat_axis=0, tiled=True
    )


def swap(block):
    return lax.ppermute(block, "section", [(0, 1), (1, 0)])


def erf(value):
    top = 3.832506856900711
    value = jnp.clip(value, -top, top)
    square = value * value
    over = jnp.float32(0.00022905065861350646)
    for term in (0.0034082910107109506, 0.050955695062380861, 0.18520832239976145, 1.128379143519084):
        over = over * square + term
    under = jnp.float32(-1.1791602954361697e-7)
    for term in (
        0.000023547966471313185,
        0.0010179625278914885,
        0.014070470171167667,
        0.11098505178285362,
        0.49746925110067538,
        1.0,
    ):
        under = under * square + term
    return value * over / under


def gelu(value):
    size = jnp.abs(value)
    inner = 1.0 / (1.0 + (0.3275911 * 0.7071067811865476) * size)
    half_tail = jnp.float32(0.5 * 1.061405429)
    for term in (-1.453152027, 1.421413741, -0.284496736, 0.254829592):
        half_tail = half_tail * inner + 0.5 * term
    half_tail = half_tail * inner * jnp.exp(-0.5 * value * value)
    return jnp.maximum(value, 0.0) - size * half_tail


def layers_kernel(
    sizes,
    stacked_hbm,
    center_hbm,
    weights_ref,
    gain_ref,
    head_ref,
    prior_ref,
    target_ref,
    out_0_ref,
    out_1_ref,
    packed_ref,
    loss_ref,
    stacked_ref,
    center_ref,
    weight_0,
    weight_1,
    hidden_ref,
    sem_s,
    sem_w,
):
    far, half, side, band, slots, parts_y, parts_x = sizes
    tall, wide, taps = stacked_ref.shape[0] - 2, stacked_ref.shape[1], stacked_ref.shape[2]
    channels = taps // 3
    bins = head_ref.shape[1]
    section = lax.axis_index("section")

    def strip(t):
        low = 0 if t == 0 else t * band + 2
        at = pl.ds(low, t * band + band + 2 - low)
        return pltpu.make_async_copy(stacked_hbm.at[at], stacked_ref.at[at], sem_s.at[t])

    strip(0).start()

    def third(i):
        at = pl.ds(i * taps, taps)
        return pltpu.make_async_copy(weights_ref.at[at], weight_0.at[at], sem_w.at[i])

    fetch_1 = pltpu.make_async_copy(weights_ref.at[pl.ds(3 * taps, 3 * taps)], weight_1, sem_w.at[3])
    for i in range(3):
        third(i).start()
    for t in range(1, tall // band):
        strip(t).start()
    fetch_center = pltpu.make_async_copy(center_hbm, center_ref, sem_w.at[4])
    fetch_center.start()
    fetch_1.start()

    row_start = lax.axis_index("sy") * side + section * half - far
    column_at = lax.axis_index("sx") * side - far + lax.broadcasted_iota(jnp.int32, (band, wide, 1), 1)
    column_in = (column_at >= 0) & (column_at < side * parts_x)
    gain = gain_ref[...].reshape(1, 1, channels)
    strip(0).wait()
    start = jnp.zeros((band * wide, channels), jnp.float32)
    for i in range(3):
        third(i).wait()
        start += jnp.dot(
            stacked_ref[i : i + band].reshape(band * wide, taps),
            weight_0[i * taps : (i + 1) * taps],
            preferred_element_type=jnp.float32,
        )
    for t in range(1, tall // band):
        strip(t).wait()
    fetch_center.wait()
    for t in range(tall // band):
        total = start if t == 0 else jnp.dot(
            jnp.concatenate(
                [stacked_ref[t * band + i : t * band + i + band] for i in range(3)], axis=2
            ).reshape(band * wide, 3 * taps),
            weight_0[...],
            preferred_element_type=jnp.float32,
        )
        total = total.reshape(band, wide, channels) + center_ref[t * band : (t + 1) * band].astype(jnp.float32)
        values = total.astype(jnp.bfloat16).astype(jnp.float32)
        if far <= t * band < far + half:
            out_0_ref[t * band - far : (t + 1) * band - far] = values[:, far : far + side].astype(jnp.bfloat16)
        mean = jnp.mean(values, axis=-1, keepdims=True)
        offset = values - mean
        spread = jnp.mean(offset * offset, axis=-1, keepdims=True)
        row_at = row_start + t * band + lax.broadcasted_iota(jnp.int32, (band, wide, 1), 0)
        inside = column_in & (row_at >= 0) & (row_at < side * parts_y)
        normed = offset * jnp.where(inside, lax.rsqrt(spread + 1e-05), 0.0) * gain
        active = gelu(normed)
        for j in range(3):
            hidden_ref[t * band : (t + 1) * band, :, j * channels : (j + 1) * channels] = active[
                :, j * far : j * far + side
            ].astype(jnp.bfloat16)

    cells = half * side
    fetch_1.wait()
    total = jnp.dot(
        jnp.concatenate([hidden_ref[i * far : i * far + half] for i in range(3)], axis=2).reshape(cells, 3 * taps),
        weight_1[...],
        preferred_element_type=jnp.float32,
    )
    flat = (total + out_0_ref[...].reshape(cells, channels).astype(jnp.float32)).astype(jnp.bfloat16)
    out_1_ref[...] = flat.reshape(half, side, channels)
    logits = jnp.dot(flat, head_ref[...], preferred_element_type=jnp.float32)
    logits = logits + prior_ref[...].astype(jnp.float32)
    shifted = logits - jnp.max(logits, axis=1, keepdims=True)
    exp_terms = jnp.exp(shifted)
    exp_total = jnp.sum(exp_terms, axis=1, keepdims=True)
    hit = target_ref[...] == lax.broadcasted_iota(jnp.int32, (cells, bins), 1)
    picked = jnp.sum(jnp.where(hit, shifted, 0.0), axis=1, keepdims=True)
    loss = jnp.sum(jnp.log(exp_total) - picked, axis=0, keepdims=True)
    delta = (exp_terms / exp_total - hit.astype(jnp.float32)).astype(jnp.bfloat16)
    gradient = lax.dot_general(
        flat, delta, (((0,), (0,)), ((), ())), preferred_element_type=jnp.float32
    )
    loss_ref[...] = jnp.broadcast_to(loss, loss_ref.shape)
    deep = packed_ref.shape[1]
    middle = channels // 2
    across = middle // deep
    left = lax.broadcasted_iota(jnp.int32, (middle, 128), 1) < 64
    for q in range(bins // 128):
        upper = gradient[:middle, q * 128 : (q + 1) * 128]
        lower = gradient[middle:, q * 128 : (q + 1) * 128]
        pair = (
            jnp.where(left, upper, pltpu.roll(lower, 64, 1)),
            jnp.where(left, pltpu.roll(upper, 64, 1), lower),
        )
        for p in range(2):
            for r in range(across):
                packed_ref[(2 * q + p) * across + r] = pair[p][r * deep : (r + 1) * deep].astype(jnp.bfloat16)


def spread_kernel(arrived_ref, loss_ref, copies_ref):
    total = jnp.sum(arrived_ref[...].astype(jnp.float32), axis=0)
    total = jnp.concatenate([total, loss_ref[...]], axis=0).astype(jnp.bfloat16)
    copies_ref[...] = jnp.broadcast_to(total[None], copies_ref.shape)


def share_kernel(arrived_ref, copies_ref):
    total = jnp.sum(arrived_ref[...].astype(jnp.float32), axis=0)
    deep = total.shape[0] - 8
    values, loss = total[:deep], total[deep : deep + 8]
    squares = jnp.sum(jnp.sum(values * values, axis=1, keepdims=True), axis=0, keepdims=True)
    turned = pltpu.roll(values, 64, 1)
    first = lax.axis_index("section") == 0
    own_left = jnp.where(first, values, turned)
    own_right = jnp.where(first, turned, values)
    tail = jnp.where(lax.broadcasted_iota(jnp.int32, (8, 128), 0) == 0, squares, loss)
    left = lax.broadcasted_iota(jnp.int32, (16, 128), 1) < 64
    block = jnp.where(left, own_left[:16], jnp.concatenate([own_right[16:deep], tail], axis=0))
    copies_ref[...] = jnp.broadcast_to(block.astype(jnp.bfloat16)[None], copies_ref.shape)


def finish_kernel(sizes, arrived_ref, step_ref, loss_ref):
    entries, cells = sizes
    arrived = arrived_ref[...].astype(jnp.float32)
    tails = jnp.sum(arrived[:, 8:], axis=0)
    scale = lax.rsqrt(tails[0:1, 127:128] * (1.0 / entries) + 1e-06)
    loss_ref[...] = jnp.broadcast_to(tails[1:2, 127:128] * (1.0 / cells), loss_ref.shape)
    deep = 24
    across = step_ref.shape[0] // deep
    left = lax.broadcasted_iota(jnp.int32, (deep, 128), 1) < 64

    def piece(s):
        block = arrived[s]
        return jnp.concatenate([block, pltpu.roll(block[:8], 64, 1)], axis=0)

    for q in range(step_ref.shape[1] // 128):
        for r in range(across):
            right = pltpu.roll(piece((2 * q + 1) * across + r), 64, 1)
            both = jnp.where(left, piece(2 * q * across + r), right) * scale
            step_ref[r * deep : (r + 1) * deep, q * 128 : (q + 1) * 128] = both


def window_kernel(sizes, left_ref, rows_ref, right_ref, gain_ref, stacked_ref, center_ref, grid_ref, active_ref):
    near, band = sizes
    rows, side, channels = rows_ref.shape
    reach = left_ref.shape[1]
    wide = side + 2 * (reach - near)
    grid_ref[...] = jnp.zeros(grid_ref.shape, jnp.float32)
    grid_ref[:, :reach] = left_ref[...].astype(jnp.float32)
    grid_ref[:, reach : reach + side] = rows_ref[...].astype(jnp.float32)
    grid_ref[:, reach + side : 2 * reach + side] = right_ref[...].astype(jnp.float32)
    gain = gain_ref[...].reshape(1, 1, channels)
    for t in range(rows // band):
        at = slice(t * band, (t + 1) * band)
        values = grid_ref[at]
        offset = values - jnp.mean(values, axis=-1, keepdims=True)
        spread = jnp.mean(offset * offset, axis=-1, keepdims=True)
        normed = offset * lax.rsqrt(spread + 1e-05) * gain
        active_ref[...] = 0.5 * normed * (1.0 + erf(normed * 0.7071067811865476))
        for j in range(3):
            stacked_ref[at, :, j * channels : (j + 1) * channels] = active_ref[
                :, j * near : j * near + wide
            ].astype(jnp.bfloat16)
    center_ref[...] = grid_ref[near : rows - near, near : near + wide].astype(jnp.bfloat16)


def per_device(
    frames, encode_weight, conv_weight, norm_gain, head_weight, prior_logits, target_bins
):
    section = lax.axis_index("section")
    first = section == 0
    parts_y = lax.axis_size("sy")
    parts_x = lax.axis_size("sx")
    parts_b = lax.axis_size("mb")
    side = frames.shape[1] // 2
    half = side // 2
    channels = encode_weight.shape[1]
    bins = head_weight.shape[1]
    near = FIRST_DILATION
    far = FIRST_DILATION * SECTION_FACTOR
    reach = near + far

    shard = conv_weight[0, 0]
    strip = copies_to(shard, "sx", parts_x)
    strip, encode_weight, norm_gain, prior_logits, target_bins, head_weight = lax.optimization_barrier(
        (strip, encode_weight, norm_gain, prior_logits, target_bins, head_weight)
    )
    gain_own = norm_gain[0, 0]
    weights = lax.all_gather(
        strip.reshape(parts_x * shard.shape[0], channels), ("section", "sy"), axis=0, tiled=True
    )
    gain_other = swap(gain_own)
    gain_0 = jnp.where(first, gain_own, gain_other)
    gain_1 = jnp.where(first, gain_other, gain_own)

    blocks = frames[0].reshape(side, 2, side, 2, frames.shape[3])
    kernel = encode_weight.reshape(2, 2, frames.shape[3], channels)
    encoded = jnp.einsum(
        "apbqc,pqco->abo", blocks, kernel, preferred_element_type=jnp.float32
    ).astype(jnp.bfloat16)

    outgoing = jnp.where(first, encoded[side - reach :], encoded[:reach])
    route = [(y, y + 1) for y in range(parts_y - 1)] + [
        (parts_y + y + 1, parts_y + y) for y in range(parts_y - 1)
    ]
    arrived = lax.ppermute(outgoing, ("section", "sy"), route)
    rows = jnp.where(
        first,
        jnp.concatenate([arrived, encoded[: half + reach]], axis=0),
        jnp.concatenate([encoded[half - reach :], arrived], axis=0),
    )
    forward = [(x, x + 1) for x in range(parts_x - 1)]
    backward = [(x + 1, x) for x in range(parts_x - 1)]
    left = lax.ppermute(rows[:, side - reach :], "sx", forward)
    right = lax.ppermute(rows[:, :reach], "sx", backward)

    tall, wide = half + 2 * far, side + 2 * far
    cells = half * side
    columns = -(-(side + 2 * reach) // 8) * 8
    stacked, center = pl.pallas_call(
        functools.partial(window_kernel, (near, 2)),
        out_shape=(
            jax.ShapeDtypeStruct((tall + 2 * near, wide, 3 * channels), jnp.bfloat16),
            jax.ShapeDtypeStruct((tall, wide, channels), jnp.bfloat16),
        ),
        scratch_shapes=[
            pltpu.VMEM((tall + 2 * near, columns, channels), jnp.float32),
            pltpu.VMEM((2, columns, channels), jnp.float32),
        ],
        compiler_params=pltpu.CompilerParams(vmem_limit_bytes=32 * 2**20),
    )(left, rows, right, gain_0.reshape(1, channels))
    prior = lax.dynamic_slice_in_dim(prior_logits[0], section * half, half, axis=0).reshape(cells, bins)
    target = lax.dynamic_slice_in_dim(target_bins[0], section * half, half, axis=0).reshape(cells, 1)
    slots = parts_x * parts_b
    deep = channels * bins // (128 * slots)
    vmem = pl.BlockSpec(memory_space=pltpu.VMEM)
    anywhere = pl.BlockSpec(memory_space=pl.ANY)
    taps = 3 * channels
    own_0, own_1, packed, loss = pl.pallas_call(
        functools.partial(layers_kernel, (far, half, side, 8, slots, parts_y, parts_x)),
        out_shape=(
            jax.ShapeDtypeStruct((half, side, channels), jnp.bfloat16),
            jax.ShapeDtypeStruct((half, side, channels), jnp.bfloat16),
            jax.ShapeDtypeStruct((slots, deep, 128), jnp.bfloat16),
            jax.ShapeDtypeStruct((8, 128), jnp.float32),
        ),
        in_specs=[anywhere, anywhere, anywhere, vmem, vmem, vmem, vmem],
        out_specs=(vmem, vmem, vmem, vmem),
        scratch_shapes=[
            pltpu.VMEM((tall + 2 * near, wide, taps), jnp.bfloat16),
            pltpu.VMEM((tall, wide, channels), jnp.bfloat16),
            pltpu.VMEM((3 * taps, channels), jnp.bfloat16),
            pltpu.VMEM((3 * taps, channels), jnp.bfloat16),
            pltpu.VMEM((tall, side, taps), jnp.bfloat16),
            pltpu.SemaphoreType.DMA((tall // 8,)),
            pltpu.SemaphoreType.DMA((5,)),
        ],
        compiler_params=pltpu.CompilerParams(vmem_limit_bytes=52 * 2**20),
        cost_estimate=pl.CostEstimate(
            flops=2 * (tall * wide + cells) * 3 * taps * channels,
            bytes_accessed=6 * taps * channels * 2,
            transcendentals=0,
        ),
    )(stacked, center, weights, gain_1.reshape(1, channels), head_weight, prior, target)

    def exchange(blocks, axes):
        return lax.all_to_all(blocks, axes, split_axis=0, concat_axis=0, tiled=True)

    small = pltpu.CompilerParams(vmem_limit_bytes=4 * 2**20)
    packed = exchange(packed, ("sx", "mb"))
    packed = pl.pallas_call(
        spread_kernel, out_shape=jax.ShapeDtypeStruct((2 * parts_y, deep + 8, 128), jnp.bfloat16), compiler_params=small
    )(packed, loss)
    packed = exchange(packed, ("section", "sy"))
    packed = pl.pallas_call(
        share_kernel, out_shape=jax.ShapeDtypeStruct((slots, 16, 128), jnp.bfloat16), compiler_params=small
    )(packed)
    packed = exchange(packed, ("sx", "mb"))
    head_step, loss = pl.pallas_call(
        functools.partial(
            finish_kernel, (channels * bins, parts_b * parts_y * parts_x * side * side)
        ),
        out_shape=(
            jax.ShapeDtypeStruct((channels // 2, bins), jnp.float32),
            jax.ShapeDtypeStruct((1, 128), jnp.float32),
        ),
        compiler_params=small,
    )(packed)
    mean_loss = loss[0, 0]

    sent = swap(jnp.where(first, own_1, own_0))
    grids = jnp.where(
        first, jnp.concatenate([own_0, sent], axis=0), jnp.concatenate([sent, own_1], axis=0)
    )[None, None]
    return (grids, head_step, mean_loss)


def solution(mesh):
    placed = (
        P("mb", "sy", "sx", None),
        P(),
        P("section", None, ("sy", "sx"), None),
        P("section", None, None),
        P(),
        P("mb", "sy", "sx", None),
        P("mb", "sy", "sx"),
    )
    return jax.shard_map(
        per_device,
        mesh=mesh,
        in_specs=placed,
        out_specs=(P("section", "mb", "sy", "sx", None), P("section", None), P()),
        check_vma=False,
    )
```

```python
import functools

import jax
import jax.numpy as jnp
from jax import lax
from jax.experimental import pallas as pl
from jax.experimental.pallas import tpu as pltpu
from jax.sharding import PartitionSpec as P

FIRST_DILATION = 1
SECTION_FACTOR = 8


def copies_to(block, axes, count):
    return lax.all_to_all(
        jnp.broadcast_to(block[None], (count,) + block.shape), axes, split_axis=0, concat_axis=0, tiled=True
    )


def swap(block):
    return lax.ppermute(block, "section", [(0, 1), (1, 0)])


def erf(value):
    top = 3.832506856900711
    value = jnp.clip(value, -top, top)
    square = value * value
    over = jnp.float32(0.00022905065861350646)
    for term in (0.0034082910107109506, 0.050955695062380861, 0.18520832239976145, 1.128379143519084):
        over = over * square + term
    under = jnp.float32(-1.1791602954361697e-7)
    for term in (
        0.000023547966471313185,
        0.0010179625278914885,
        0.014070470171167667,
        0.11098505178285362,
        0.49746925110067538,
        1.0,
    ):
        under = under * square + term
    return value * over / under


def gelu(value):
    size = jnp.abs(value)
    inner = 1.0 / (1.0 + (0.3275911 * 0.7071067811865476) * size)
    half_tail = jnp.float32(0.5 * 1.061405429)
    for term in (-1.453152027, 1.421413741, -0.284496736, 0.254829592):
        half_tail = half_tail * inner + 0.5 * term
    half_tail = half_tail * inner * jnp.exp(-0.5 * value * value)
    return jnp.maximum(value, 0.0) - size * half_tail


def layers_kernel(
    sizes,
    stacked_hbm,
    center_hbm,
    weights_ref,
    gain_ref,
    head_ref,
    prior_ref,
    target_ref,
    out_0_ref,
    out_1_ref,
    packed_ref,
    loss_ref,
    stacked_ref,
    center_ref,
    weight_0,
    weight_1,
    hidden_ref,
    sem_s,
    sem_w,
):
    far, half, side, band, slots, parts_y, parts_x = sizes
    tall, wide, taps = stacked_ref.shape[0] - 2, stacked_ref.shape[1], stacked_ref.shape[2]
    channels = taps // 3
    bins = head_ref.shape[1]
    section = lax.axis_index("section")

    def strip(t):
        low = 0 if t == 0 else t * band + 2
        at = pl.ds(low, t * band + band + 2 - low)
        return pltpu.make_async_copy(stacked_hbm.at[at], stacked_ref.at[at], sem_s.at[t])

    strip(0).start()

    def third(i):
        at = pl.ds(i * taps, taps)
        return pltpu.make_async_copy(weights_ref.at[at], weight_0.at[at], sem_w.at[i])

    fetch_1 = pltpu.make_async_copy(weights_ref.at[pl.ds(3 * taps, 3 * taps)], weight_1, sem_w.at[3])
    for i in range(3):
        third(i).start()
    for t in range(1, tall // band):
        strip(t).start()
    fetch_center = pltpu.make_async_copy(center_hbm, center_ref, sem_w.at[4])
    fetch_center.start()
    fetch_1.start()

    row_start = lax.axis_index("sy") * side + section * half - far
    column_at = lax.axis_index("sx") * side - far + lax.broadcasted_iota(jnp.int32, (band, wide, 1), 1)
    column_in = (column_at >= 0) & (column_at < side * parts_x)
    gain = gain_ref[...].reshape(1, 1, channels)
    strip(0).wait()
    start = jnp.zeros((band * wide, channels), jnp.float32)
    for i in range(3):
        third(i).wait()
        start += jnp.dot(
            stacked_ref[i : i + band].reshape(band * wide, taps),
            weight_0[i * taps : (i + 1) * taps],
            preferred_element_type=jnp.float32,
        )
    for t in range(1, tall // band):
        strip(t).wait()
    fetch_center.wait()
    for t in range(tall // band):
        total = start if t == 0 else jnp.dot(
            jnp.concatenate(
                [stacked_ref[t * band + i : t * band + i + band] for i in range(3)], axis=2
            ).reshape(band * wide, 3 * taps),
            weight_0[...],
            preferred_element_type=jnp.float32,
        )
        total = total.reshape(band, wide, channels) + center_ref[t * band : (t + 1) * band].astype(jnp.float32)
        values = total.astype(jnp.bfloat16).astype(jnp.float32)
        if far <= t * band < far + half:
            out_0_ref[t * band - far : (t + 1) * band - far] = values[:, far : far + side].astype(jnp.bfloat16)
        mean = jnp.mean(values, axis=-1, keepdims=True)
        offset = values - mean
        spread = jnp.mean(offset * offset, axis=-1, keepdims=True)
        row_at = row_start + t * band + lax.broadcasted_iota(jnp.int32, (band, wide, 1), 0)
        inside = column_in & (row_at >= 0) & (row_at < side * parts_y)
        normed = offset * jnp.where(inside, lax.rsqrt(spread + 1e-05), 0.0) * gain
        active = gelu(normed)
        for j in range(3):
            hidden_ref[t * band : (t + 1) * band, :, j * channels : (j + 1) * channels] = active[
                :, j * far : j * far + side
            ].astype(jnp.bfloat16)

    cells = half * side
    fetch_1.wait()
    total = jnp.dot(
        jnp.concatenate([hidden_ref[i * far : i * far + half] for i in range(3)], axis=2).reshape(cells, 3 * taps),
        weight_1[...],
        preferred_element_type=jnp.float32,
    )
    flat = (total + out_0_ref[...].reshape(cells, channels).astype(jnp.float32)).astype(jnp.bfloat16)
    out_1_ref[...] = flat.reshape(half, side, channels)
    logits = jnp.dot(flat, head_ref[...], preferred_element_type=jnp.float32)
    logits = logits + prior_ref[...].astype(jnp.float32)
    shifted = logits - jnp.max(logits, axis=1, keepdims=True)
    exp_terms = jnp.exp(shifted)
    exp_total = jnp.sum(exp_terms, axis=1, keepdims=True)
    hit = target_ref[...] == lax.broadcasted_iota(jnp.int32, (cells, bins), 1)
    picked = jnp.sum(jnp.where(hit, shifted, 0.0), axis=1, keepdims=True)
    loss = jnp.sum(jnp.log(exp_total) - picked, axis=0, keepdims=True)
    softmax = exp_terms * (1.0 / exp_total)
    delta = jnp.where(hit, softmax - 1.0, softmax).astype(jnp.bfloat16)
    gradient = lax.dot_general(
        flat, delta, (((0,), (0,)), ((), ())), preferred_element_type=jnp.float32
    )
    loss_ref[...] = jnp.broadcast_to(loss, loss_ref.shape)
    deep = packed_ref.shape[1]
    middle = channels // 2
    across = middle // deep
    left = lax.broadcasted_iota(jnp.int32, (middle, 128), 1) < 64
    for q in range(bins // 128):
        upper = gradient[:middle, q * 128 : (q + 1) * 128]
        lower = gradient[middle:, q * 128 : (q + 1) * 128]
        pair = (
            jnp.where(left, upper, pltpu.roll(lower, 64, 1)),
            jnp.where(left, pltpu.roll(upper, 64, 1), lower),
        )
        for p in range(2):
            for r in range(across):
                packed_ref[(2 * q + p) * across + r] = pair[p][r * deep : (r + 1) * deep].astype(jnp.bfloat16)


def spread_kernel(arrived_ref, loss_ref, copies_ref):
    total = jnp.sum(arrived_ref[...].astype(jnp.float32), axis=0)
    total = jnp.concatenate([total, loss_ref[...]], axis=0).astype(jnp.bfloat16)
    copies_ref[...] = jnp.broadcast_to(total[None], copies_ref.shape)


def share_kernel(arrived_ref, copies_ref):
    total = jnp.sum(arrived_ref[...].astype(jnp.float32), axis=0)
    deep = total.shape[0] - 8
    values, loss = total[:deep], total[deep : deep + 8]
    squares = jnp.sum(jnp.sum(values * values, axis=1, keepdims=True), axis=0, keepdims=True)
    turned = pltpu.roll(values, 64, 1)
    first = lax.axis_index("section") == 0
    own_left = jnp.where(first, values, turned)
    own_right = jnp.where(first, turned, values)
    tail = jnp.where(lax.broadcasted_iota(jnp.int32, (8, 128), 0) == 0, squares, loss)
    left = lax.broadcasted_iota(jnp.int32, (16, 128), 1) < 64
    block = jnp.where(left, own_left[:16], jnp.concatenate([own_right[16:deep], tail], axis=0))
    copies_ref[...] = jnp.broadcast_to(block.astype(jnp.bfloat16)[None], copies_ref.shape)


def finish_kernel(sizes, arrived_ref, step_ref, loss_ref):
    entries, cells = sizes
    arrived = arrived_ref[...].astype(jnp.float32)
    tails = jnp.sum(arrived[:, 8:], axis=0)
    scale = lax.rsqrt(tails[0:1, 127:128] * (1.0 / entries) + 1e-06)
    loss_ref[...] = jnp.broadcast_to(tails[1:2, 127:128] * (1.0 / cells), loss_ref.shape)
    deep = 24
    across = step_ref.shape[0] // deep
    left = lax.broadcasted_iota(jnp.int32, (deep, 128), 1) < 64

    def piece(s):
        block = arrived[s]
        return jnp.concatenate([block, pltpu.roll(block[:8], 64, 1)], axis=0)

    for q in range(step_ref.shape[1] // 128):
        for r in range(across):
            right = pltpu.roll(piece((2 * q + 1) * across + r), 64, 1)
            both = jnp.where(left, piece(2 * q * across + r), right) * scale
            step_ref[r * deep : (r + 1) * deep, q * 128 : (q + 1) * 128] = both


def window_kernel(sizes, left_ref, rows_ref, right_ref, gain_ref, stacked_ref, center_ref, grid_ref, active_ref):
    near, band = sizes
    rows, side, channels = rows_ref.shape
    reach = left_ref.shape[1]
    wide = side + 2 * (reach - near)
    grid_ref[...] = jnp.zeros(grid_ref.shape, jnp.float32)
    grid_ref[:, :reach] = left_ref[...].astype(jnp.float32)
    grid_ref[:, reach : reach + side] = rows_ref[...].astype(jnp.float32)
    grid_ref[:, reach + side : 2 * reach + side] = right_ref[...].astype(jnp.float32)
    gain = gain_ref[...].reshape(1, 1, channels)
    for t in range(rows // band):
        at = slice(t * band, (t + 1) * band)
        values = grid_ref[at]
        offset = values - jnp.mean(values, axis=-1, keepdims=True)
        spread = jnp.mean(offset * offset, axis=-1, keepdims=True)
        normed = offset * lax.rsqrt(spread + 1e-05) * gain
        active_ref[...] = 0.5 * normed * (1.0 + erf(normed * 0.7071067811865476))
        for j in range(3):
            stacked_ref[at, :, j * channels : (j + 1) * channels] = active_ref[
                :, j * near : j * near + wide
            ].astype(jnp.bfloat16)
    center_ref[...] = grid_ref[near : rows - near, near : near + wide].astype(jnp.bfloat16)


def per_device(
    frames, encode_weight, conv_weight, norm_gain, head_weight, prior_logits, target_bins
):
    section = lax.axis_index("section")
    first = section == 0
    parts_y = lax.axis_size("sy")
    parts_x = lax.axis_size("sx")
    parts_b = lax.axis_size("mb")
    side = frames.shape[1] // 2
    half = side // 2
    channels = encode_weight.shape[1]
    bins = head_weight.shape[1]
    near = FIRST_DILATION
    far = FIRST_DILATION * SECTION_FACTOR
    reach = near + far

    shard = conv_weight[0, 0]
    strip = copies_to(shard, "sx", parts_x)
    strip, encode_weight, norm_gain, prior_logits, target_bins, head_weight = lax.optimization_barrier(
        (strip, encode_weight, norm_gain, prior_logits, target_bins, head_weight)
    )
    gain_own = norm_gain[0, 0]
    weights = lax.all_gather(
        strip.reshape(parts_x * shard.shape[0], channels), ("section", "sy"), axis=0, tiled=True
    )
    gain_other = swap(gain_own)
    gain_0 = jnp.where(first, gain_own, gain_other)
    gain_1 = jnp.where(first, gain_other, gain_own)

    blocks = frames[0].reshape(side, 2, side, 2, frames.shape[3])
    kernel = encode_weight.reshape(2, 2, frames.shape[3], channels)
    encoded = jnp.einsum(
        "apbqc,pqco->abo", blocks, kernel, preferred_element_type=jnp.float32
    ).astype(jnp.bfloat16)

    outgoing = jnp.where(first, encoded[side - reach :], encoded[:reach])
    route = [(y, y + 1) for y in range(parts_y - 1)] + [
        (parts_y + y + 1, parts_y + y) for y in range(parts_y - 1)
    ]
    arrived = lax.ppermute(outgoing, ("section", "sy"), route)
    rows = jnp.where(
        first,
        jnp.concatenate([arrived, encoded[: half + reach]], axis=0),
        jnp.concatenate([encoded[half - reach :], arrived], axis=0),
    )
    forward = [(x, x + 1) for x in range(parts_x - 1)]
    backward = [(x + 1, x) for x in range(parts_x - 1)]
    left = lax.ppermute(rows[:, side - reach :], "sx", forward)
    right = lax.ppermute(rows[:, :reach], "sx", backward)

    tall, wide = half + 2 * far, side + 2 * far
    cells = half * side
    columns = -(-(side + 2 * reach) // 8) * 8
    stacked, center = pl.pallas_call(
        functools.partial(window_kernel, (near, 2)),
        out_shape=(
            jax.ShapeDtypeStruct((tall + 2 * near, wide, 3 * channels), jnp.bfloat16),
            jax.ShapeDtypeStruct((tall, wide, channels), jnp.bfloat16),
        ),
        scratch_shapes=[
            pltpu.VMEM((tall + 2 * near, columns, channels), jnp.float32),
            pltpu.VMEM((2, columns, channels), jnp.float32),
        ],
        compiler_params=pltpu.CompilerParams(vmem_limit_bytes=32 * 2**20),
    )(left, rows, right, gain_0.reshape(1, channels))
    prior = lax.dynamic_slice_in_dim(prior_logits[0], section * half, half, axis=0).reshape(cells, bins)
    target = lax.dynamic_slice_in_dim(target_bins[0], section * half, half, axis=0).reshape(cells, 1)
    slots = parts_x * parts_b
    deep = channels * bins // (128 * slots)
    vmem = pl.BlockSpec(memory_space=pltpu.VMEM)
    anywhere = pl.BlockSpec(memory_space=pl.ANY)
    taps = 3 * channels
    own_0, own_1, packed, loss = pl.pallas_call(
        functools.partial(layers_kernel, (far, half, side, 8, slots, parts_y, parts_x)),
        out_shape=(
            jax.ShapeDtypeStruct((half, side, channels), jnp.bfloat16),
            jax.ShapeDtypeStruct((half, side, channels), jnp.bfloat16),
            jax.ShapeDtypeStruct((slots, deep, 128), jnp.bfloat16),
            jax.ShapeDtypeStruct((8, 128), jnp.float32),
        ),
        in_specs=[anywhere, anywhere, anywhere, vmem, vmem, vmem, vmem],
        out_specs=(vmem, vmem, vmem, vmem),
        scratch_shapes=[
            pltpu.VMEM((tall + 2 * near, wide, taps), jnp.bfloat16),
            pltpu.VMEM((tall, wide, channels), jnp.bfloat16),
            pltpu.VMEM((3 * taps, channels), jnp.bfloat16),
            pltpu.VMEM((3 * taps, channels), jnp.bfloat16),
            pltpu.VMEM((tall, side, taps), jnp.bfloat16),
            pltpu.SemaphoreType.DMA((tall // 8,)),
            pltpu.SemaphoreType.DMA((5,)),
        ],
        compiler_params=pltpu.CompilerParams(vmem_limit_bytes=52 * 2**20),
        cost_estimate=pl.CostEstimate(
            flops=2 * (tall * wide + cells) * 3 * taps * channels,
            bytes_accessed=6 * taps * channels * 2,
            transcendentals=0,
        ),
    )(stacked, center, weights, gain_1.reshape(1, channels), head_weight, prior, target)

    def exchange(blocks, axes):
        return lax.all_to_all(blocks, axes, split_axis=0, concat_axis=0, tiled=True)

    small = pltpu.CompilerParams(vmem_limit_bytes=4 * 2**20)
    packed = exchange(packed, ("sx", "mb"))
    packed = pl.pallas_call(
        spread_kernel, out_shape=jax.ShapeDtypeStruct((2 * parts_y, deep + 8, 128), jnp.bfloat16), compiler_params=small
    )(packed, loss)
    packed = exchange(packed, ("section", "sy"))
    packed = pl.pallas_call(
        share_kernel, out_shape=jax.ShapeDtypeStruct((slots, 16, 128), jnp.bfloat16), compiler_params=small
    )(packed)
    packed = exchange(packed, ("sx", "mb"))
    head_step, loss = pl.pallas_call(
        functools.partial(
            finish_kernel, (channels * bins, parts_b * parts_y * parts_x * side * side)
        ),
        out_shape=(
            jax.ShapeDtypeStruct((channels // 2, bins), jnp.float32),
            jax.ShapeDtypeStruct((1, 128), jnp.float32),
        ),
        compiler_params=small,
    )(packed)
    mean_loss = loss[0, 0]

    sent = swap(jnp.where(first, own_1, own_0))
    grids = jnp.where(
        first, jnp.concatenate([own_0, sent], axis=0), jnp.concatenate([sent, own_1], axis=0)
    )[None, None]
    return (grids, head_step, mean_loss)


def solution(mesh):
    placed = (
        P("mb", "sy", "sx", None),
        P(),
        P("section", None, ("sy", "sx"), None),
        P("section", None, None),
        P(),
        P("mb", "sy", "sx", None),
        P("mb", "sy", "sx"),
    )
    return jax.shard_map(
        per_device,
        mesh=mesh,
        in_specs=placed,
        out_specs=(P("section", "mb", "sy", "sx", None), P("section", None), P()),
        check_vma=False,
    )
```
